128 devices in a mesh: seq: 16 (over y_hi, z, core), tp: 8 (over y_lo, x).
Axes of the slice: x: 4, y: 4 (y_hi: 2, y_lo: 2; y = y_hi * 2 + y_lo), z: 4, core: 2. Of those that a mesh axis runs over, the one named last changes fastest.
Arguments:
- queries: bfloat16 [1024, 8192], P(None, 'tp'), may hold values from -80 to 80
- cache: bfloat16 [2, 16, 16384, 1024], P(None, None, 'seq', 'tp'), may hold values from -6 to 6
- draft_kv: bfloat16 [2, 1024, 1024], P(None, 'seq', 'tp'), may hold values from -9 to 9
- out_weight: bfloat16 [8192, 8192], P('tp', 'seq'), may hold values from -0.0625 to 0.0625
- lengths: int32 [16], replicated, may hold values from 1020 to 16376, as said below
- parents: int32 [16, 64], replicated, may hold values from -1 to 62, as said below
- path: int32 [16, 8], replicated, may hold values from 0 to 63, as said below
- accepted: int32 [16], replicated, may hold values from 1 to 8
Outputs:
- attn_out: bfloat16 [1024, 8192], P('tp', 'seq')
- new_cache: bfloat16 [2, 16, 16384, 1024], P(None, None, 'seq', 'tp')
The draws below stay inside these ranges and needn't reach their ends.
Inputs may be any that keep to these rules, and one draw needn't show every extreme that they name: `lengths`: request r belongs to tenant t = r mod 4; a request of tenant t holds at most 16384 // 8 * 2 ** t - 8 tokens and at least half of that, and the first request of each tenant holds exactly that many. `parents`: node 0 is the root, with parent -1; every other node i has its parent among the nodes i - 7 to i - 1. `path`: for each request, the nodes of one branch of its tree, each the parent of the next, the last being node 63.
All inputs are finite; a program needn't handle non-finite values.
Results may differ from the reference program's by a relative error of at most 0.0051.
Values may be sent and summed in bfloat16 or wider, within the bound.
A program may use at most 192 MiB of HBM per device.

```python
import jax
import jax.numpy as jnp
from jax import lax

D = 8192
HEADS = 64
KV_HEADS = 8
HEAD = 128
Q = 64
ACC = 8
CACHE_DEV = 1024
REQUESTS = 16
LMAX = 16384
ROWS = 1024
SPAN = 7


def draw_queries(key, part):
    drawn = jnp.clip(jax.random.normal(jax.random.fold_in(key, 3), (ROWS, HEADS * HEAD), jnp.float32), -6.0, 6.0) * 2.5
    return drawn.astype(jnp.bfloat16)


def draw_cache(key, part):
    drawn = jnp.clip(jax.random.normal(jax.random.fold_in(key, 5), (2, REQUESTS, LMAX, KV_HEADS * HEAD), jnp.float32), -6.0, 6.0)
    return drawn.astype(jnp.bfloat16)


def draw_lengths(key, part):
    tenant = jnp.arange(REQUESTS, dtype=jnp.int32) % 4
    factors = jnp.array([1, 2, 4, 8], jnp.int32)
    ceiling = LMAX // 8 * factors[tenant] - ACC
    drawn = jax.random.randint(jax.random.fold_in(key, 9), (REQUESTS,), ceiling // 2, ceiling + 1)
    return jnp.where(jnp.arange(REQUESTS, dtype=jnp.int32) < 4, ceiling, drawn).astype(jnp.int32)


def tree_parents(key):
    node_ids = jnp.arange(Q, dtype=jnp.int32)
    reach_back = jnp.maximum(jnp.minimum(node_ids, SPAN), 1)
    step_back = jax.random.randint(jax.random.fold_in(key, 11), (REQUESTS, Q), 1, reach_back[None, :] + 1)
    return jnp.where(node_ids[None, :] == 0, -1, node_ids[None, :] - step_back).astype(jnp.int32)


def draw_parents(key, part):
    return tree_parents(key)


def draw_path(key, part):
    parent = tree_parents(key)

    def climb_up(current, unused):
        next_node = jnp.take_along_axis(parent, current[:, None], axis=1)[:, 0]
        return (next_node, current)
    deepest = jnp.full((REQUESTS,), Q - 1, jnp.int32)
    final_node, climbed = lax.scan(climb_up, deepest, None, length=ACC)
    return climbed[::-1].T.astype(jnp.int32)


def set_ends(values, stream_key, low, high):
    place = [jax.random.randint(jax.random.fold_in(stream_key, axis), (), 0, length) for axis, length in enumerate(values.shape)]
    longest = values.shape.index(max(values.shape))
    next_to = place[:longest] + [(place[longest] + 1) % values.shape[longest]] + place[longest + 1:]
    return values.at[tuple(place)].set(low).at[tuple(next_to)].set(high)


def level_of(key, shape, split, least, top_value):
    level, own = 1.0, jax.random.fold_in(key, 6)
    for axis_at, parts in split:
        steps = jnp.exp(jax.random.uniform(jax.random.fold_in(own, axis_at), (parts,), jnp.float32, least / len(split), top_value / len(split)))
        level = level * jnp.repeat(steps, shape[axis_at] // parts).reshape([-1 if axis == axis_at else 1 for axis in range(len(shape))])
    return level


def normal_values(stream_key, extent, deviation, most, cuts=(), kind=jnp.bfloat16):
    values = deviation * jax.random.normal(stream_key, extent, jnp.float32)
    if cuts:
        values = values * level_of(stream_key, extent, cuts, -0.22, 0.18)
    return jnp.clip(values, -most, most).astype(kind)


def setup_inputs(seed: int = 0) -> dict:
    keys = jax.random.split(jax.random.key(seed), 9)
    queries = draw_queries(jax.random.fold_in(keys[8], 71), 0)
    cache = draw_cache(jax.random.fold_in(keys[8], 71), 0)
    draft_kv = normal_values(keys[2], (2, ROWS, KV_HEADS * HEAD), 1.5, 9.0, ((1, 16), (2, 8)))
    out_weight = normal_values(keys[3], (D, D), D ** -0.5, 0.0625, ((0, 8), (1, 16)))
    lengths = draw_lengths(jax.random.fold_in(keys[8], 71), 0)
    parents = draw_parents(jax.random.fold_in(keys[8], 71), 0)
    path = draw_path(jax.random.fold_in(keys[8], 71), 0)
    accepted = set_ends(jax.random.randint(keys[7], (REQUESTS,), 1, ACC + 1), jax.random.fold_in(keys[7], 1), 1, ACC).astype(jnp.int32)
    return {"queries": queries, "cache": cache, "draft_kv": draft_kv, "out_weight": out_weight, "lengths": lengths, "parents": parents, "path": path, "accepted": accepted}


masked_score = -1.0e30


def ancestors(parents):
    node_count = parents.shape[1]
    node_ids = jnp.arange(node_count, dtype=jnp.int32)
    step_map = (parents[:, :, None] == node_ids[None, None, :]).astype(jnp.float32)
    identity = jnp.broadcast_to(jnp.eye(node_count, dtype=jnp.float32), step_map.shape)
    reached = jnp.minimum(identity + step_map, 1.0)
    for doubling in range((node_count - 1).bit_length()):
        squared = jnp.einsum("nij,njk->nik", reached, reached, precision=lax.Precision.HIGHEST)
        reached = jnp.minimum(squared, 1.0)
    return reached


def partial_block(query_rows, key_rows, value_rows, alive_mask):
    scores = jnp.einsum("qkge,pke->qkgp", query_rows.astype(jnp.float32), key_rows.astype(jnp.float32)) * (HEAD ** -0.5)
    masked = jnp.where(alive_mask, scores, masked_score)
    peak_score = jnp.max(masked, axis=-1)
    weights = jnp.where(alive_mask, jnp.exp(scores - peak_score[..., None]), 0.0)
    denominator = jnp.sum(weights, axis=-1)
    rounded = lax.optimization_barrier(weights.astype(jnp.bfloat16))
    weighted = jnp.einsum("qkgp,pke->qkge", rounded.astype(jnp.float32), value_rows.astype(jnp.float32))
    return peak_score, denominator, weighted


def join(former, latter):
    peak_score = jnp.maximum(former[0], latter[0])
    weight_former = jnp.exp(former[0] - peak_score)
    weight_latter = jnp.exp(latter[0] - peak_score)
    denominator = former[1] * weight_former + latter[1] * weight_latter
    weighted = former[2] * weight_former[..., None] + latter[2] * weight_latter[..., None]
    return peak_score, denominator, weighted


def reference(queries, cache, draft_kv, out_weight, lengths, parents, path, accepted):
    requests = lengths.shape[0]
    group_size = HEADS // KV_HEADS
    blocks = LMAX // CACHE_DEV
    reach = ancestors(parents)
    query_all = queries.reshape(requests, Q, KV_HEADS, group_size, HEAD)
    key_cache = cache[0].reshape(requests, blocks, CACHE_DEV, KV_HEADS, HEAD)
    value_cache = cache[1].reshape(requests, blocks, CACHE_DEV, KV_HEADS, HEAD)
    draft_table = draft_kv.reshape(2, requests, Q, KV_HEADS, HEAD)

    def one_request(inputs):
        query_rows, key_blocks, value_blocks, draft_keys, draft_values, reach_rows, length = inputs
        running = partial_block(query_rows, draft_keys, draft_values, reach_rows[:, None, None, :] > 0.5)

        def add_block(current, block_data):
            key_rows, value_rows, row_start = block_data
            alive_mask = (row_start + jnp.arange(CACHE_DEV, dtype=jnp.int32)) < length
            return join(current, partial_block(query_rows, key_rows, value_rows, alive_mask[None, None, None, :])), None

        starts = jnp.arange(blocks, dtype=jnp.int32) * CACHE_DEV
        running, unused = lax.scan(add_block, running, (key_blocks, value_blocks, starts))
        return (running[2] / running[1][..., None]).astype(jnp.bfloat16)

    attended = lax.map(one_request, (query_all, key_cache, value_cache, draft_table[0], draft_table[1], reach, lengths))
    attended = attended.reshape(requests * Q, HEADS * HEAD)
    attn_out = jnp.dot(attended, out_weight, preferred_element_type=jnp.float32).astype(jnp.bfloat16)

    draft_flat = draft_kv.reshape(2, requests, Q, KV_HEADS * HEAD)
    selector = (path[:, :, None] == jnp.arange(Q, dtype=jnp.int32)[None, None, :]).astype(jnp.float32)
    chosen = jnp.einsum("naq,xnqd->xnad", selector, draft_flat.astype(jnp.float32)).astype(jnp.bfloat16)
    slot_ids = lengths[:, None] + jnp.arange(ACC, dtype=jnp.int32)[None, :]
    owner_ids = jnp.broadcast_to(jnp.arange(requests, dtype=jnp.int32)[:, None], slot_ids.shape)
    previous = cache[:, owner_ids, slot_ids]
    keep_mask = (jnp.arange(ACC, dtype=jnp.int32)[None, :] < accepted[:, None])[None, :, :, None]
    new_cache = cache.at[:, owner_ids, slot_ids].set(jnp.where(keep_mask, chosen, previous))
    return attn_out, new_cache
```

```python
import functools

import jax
import jax.numpy as jnp
from jax import lax
from jax.experimental import pallas as pl
from jax.experimental.pallas import tpu as pltpu
from jax.sharding import PartitionSpec as P

HEAD = 128
Q = 64
ACC = 8
MESH = pl.DeviceIdType.MESH
SCALE = HEAD**-0.5 * 1.4426950408889634
DEAD = -1e30
CHUNK = 256
WINDOW = 32


def stacked_heads(rows):
    heads = rows.shape[1] // HEAD
    return jnp.concatenate([rows[:, h * HEAD : (h + 1) * HEAD] for h in range(heads)], axis=0)


def attend_kernel(len_ref, q_ref, kv_ref, o_ref, st_ref, nc_ref, s_ref, acc_ref, max_ref, sem):
    span = kv_ref.shape[2]
    chunks = span // CHUNK
    width = s_ref.shape[1]
    r = pl.program_id(0)
    live = jnp.clip(len_ref[r] - lax.axis_index("seq") * span, 0, span)
    copy = pltpu.make_async_copy(kv_ref, nc_ref.at[:, pl.ds(r, 1)], sem)
    copy.start()

    def scores(at):
        return lax.dot_general(
            kv_ref[0, 0, pl.ds(at, CHUNK), :],
            stacked_heads(q_ref[...]),
            (((1,), (1,)), ((), ())),
            preferred_element_type=jnp.float32,
        )

    def folded(s):
        return jnp.max(s.reshape(CHUNK // 8, 8, width), axis=0)

    def weighted(at, p):
        values = kv_ref[1, 0, pl.ds(at, CHUNK), :].T
        values = jnp.concatenate([values, jnp.ones((16, CHUNK), values.dtype)], axis=0)
        return jnp.dot(values, p, preferred_element_type=jnp.float32)

    def publish(peak, acc):
        o_ref[0] = acc[:HEAD].astype(o_ref.dtype)
        st_ref[0, 0:1] = peak
        st_ref[0, 1:2] = acc[HEAD : HEAD + 1]

    @pl.when(live == 0)
    def _():
        publish(jnp.full((1, width), DEAD, jnp.float32), jnp.zeros((HEAD + 16, width), jnp.float32))

    @pl.when(live == span)
    def _():
        peak = None
        for c in range(chunks):
            s = scores(c * CHUNK)
            s_ref[pl.ds(c * CHUNK, CHUNK), :] = s
            peak = folded(s) if peak is None else jnp.maximum(peak, folded(s))
        peak = jnp.max(peak, axis=0, keepdims=True) * SCALE
        acc = None
        for c in range(chunks):
            p = jnp.exp2(s_ref[pl.ds(c * CHUNK, CHUNK), :] * SCALE - peak).astype(jnp.bfloat16)
            term = weighted(c * CHUNK, p)
            acc = term if acc is None else acc + term
        publish(peak, acc)

    @pl.when((live > 0) & (live < span))
    def _():
        used = (live + CHUNK - 1) // CHUNK
        max_ref[...] = jnp.full_like(max_ref, DEAD)
        acc_ref[...] = jnp.zeros_like(acc_ref)

        def first(c, _):
            at = pl.multiple_of(c * CHUNK, CHUNK)
            row = lax.broadcasted_iota(jnp.int32, (CHUNK, width), 0) + at
            s = jnp.where(row < live, scores(at), DEAD)
            s_ref[pl.ds(at, CHUNK), :] = s
            max_ref[...] = jnp.maximum(max_ref[...], folded(s))
            return 0

        lax.fori_loop(0, used, first, 0)
        peak = jnp.max(max_ref[...], axis=0, keepdims=True) * SCALE

        def second(c, _):
            at = pl.multiple_of(c * CHUNK, CHUNK)
            row = lax.broadcasted_iota(jnp.int32, (CHUNK, width), 0) + at
            p = jnp.exp2(s_ref[pl.ds(at, CHUNK), :] * SCALE - peak)
            p = jnp.where(row < live, p, 0.0).astype(jnp.bfloat16)
            acc_ref[...] += weighted(at, p)
            return 0

        lax.fori_loop(0, used, second, 0)
        publish(peak, acc_ref[...])

    copy.wait()


def attend(lengths, queries, cache):
    requests, span = cache.shape[1], cache.shape[2]
    width = queries.shape[1] // HEAD * Q
    return pl.pallas_call(
        attend_kernel,
        out_shape=(
            jax.ShapeDtypeStruct((requests, HEAD, width), jnp.bfloat16),
            jax.ShapeDtypeStruct((requests, 8, width), jnp.float32),
            jax.ShapeDtypeStruct(cache.shape, cache.dtype),
        ),
        grid_spec=pltpu.PrefetchScalarGridSpec(
            num_scalar_prefetch=1,
            grid=(requests,),
            in_specs=[
                pl.BlockSpec((Q, queries.shape[1]), lambda r, n: (r, 0)),
                pl.BlockSpec((2, 1, span, HEAD), lambda r, n: (0, r, 0, 0)),
            ],
            out_specs=(
                pl.BlockSpec((1, HEAD, width), lambda r, n: (r, 0, 0)),
                pl.BlockSpec((1, 8, width), lambda r, n: (r, 0, 0)),
                pl.BlockSpec(memory_space=pl.ANY),
            ),
            scratch_shapes=[
                pltpu.VMEM((span, width), jnp.float32),
                pltpu.VMEM((HEAD + 16, width), jnp.float32),
                pltpu.VMEM((8, width), jnp.float32),
                pltpu.SemaphoreType.DMA,
            ],
        ),
        compiler_params=pltpu.CompilerParams(vmem_limit_bytes=32 << 20),
        name="attend",
    )(lengths, queries, cache)


def commit_kernel(len_ref, path_ref, acc_ref, draft_ref, nc_in, nc_ref, win_ref, load_sem, store_sem):
    requests, span = nc_ref.shape[1], nc_ref.shape[2]
    base = lax.axis_index("seq") * span

    def place(r):
        off = len_ref[r] - base
        hit = (off + acc_ref[r] > 0) & (off < span)
        start = pl.multiple_of(jnp.clip(off // 16 * 16, 0, span - WINDOW), 16)
        return off, hit, start

    def load(r, start):
        return pltpu.make_async_copy(
            nc_ref.at[:, r, pl.ds(start, WINDOW), :], win_ref.at[r], load_sem.at[r]
        )

    def store(r, start):
        return pltpu.make_async_copy(
            win_ref.at[r], nc_ref.at[:, r, pl.ds(start, WINDOW), :], store_sem.at[r]
        )

    def begin(r, _):
        off, hit, start = place(r)

        @pl.when(hit)
        def _():
            load(r, start).start()

        return 0

    def change(r, _):
        off, hit, start = place(r)

        @pl.when(hit)
        def _():
            row = lax.broadcasted_iota(jnp.int32, (WINDOW, Q), 0) + (start - off)
            node = lax.broadcasted_iota(jnp.int32, (WINDOW, Q), 1)
            pick = jnp.zeros((WINDOW, Q), jnp.float32)
            for j in range(ACC):
                pick = jnp.where((row == j) & (node == path_ref[r, j]), 1.0, pick)
            slot = lax.broadcasted_iota(jnp.int32, (WINDOW, HEAD), 0) + (start - off)
            fresh = (slot >= 0) & (slot < acc_ref[r])
            load(r, start).wait()
            for x in range(2):
                rows = jnp.dot(
                    pick.astype(jnp.bfloat16),
                    draft_ref[x, pl.ds(pl.multiple_of(r * Q, Q), Q), :],
                    preferred_element_type=jnp.float32,
                )
                old = win_ref[r, x].astype(jnp.float32)
                win_ref[r, x] = jnp.where(fresh, rows, old).astype(jnp.bfloat16)
            store(r, start).start()

        return 0

    def end(r, _):
        off, hit, start = place(r)

        @pl.when(hit)
        def _():
            store(r, start).wait()

        return 0

    lax.fori_loop(0, requests, begin, 0)
    lax.fori_loop(0, requests, change, 0)
    lax.fori_loop(0, requests, end, 0)


def commit(lengths, path, accepted, drafts, new_cache):
    requests = new_cache.shape[1]
    return pl.pallas_call(
        commit_kernel,
        out_shape=jax.ShapeDtypeStruct(new_cache.shape, new_cache.dtype),
        in_specs=[pl.BlockSpec(memory_space=pltpu.SMEM)] * 3
        + [pl.BlockSpec(memory_space=pltpu.VMEM), pl.BlockSpec(memory_space=pl.ANY)],
        out_specs=pl.BlockSpec(memory_space=pl.ANY),
        scratch_shapes=[
            pltpu.VMEM((requests, 2, WINDOW, HEAD), jnp.bfloat16),
            pltpu.SemaphoreType.DMA((requests,)),
            pltpu.SemaphoreType.DMA((requests,)),
        ],
        input_output_aliases={4: 0},
        name="commit",
    )(lengths, path, accepted, drafts, new_cache)


def closure(parents):
    nodes = jnp.arange(Q, dtype=jnp.int32)
    reached = ((parents[:, None] == nodes[None, :]) | (nodes[:, None] == nodes[None, :])).astype(jnp.bfloat16)
    for _ in range((Q - 1).bit_length()):
        reached = jnp.minimum(jnp.dot(reached, reached, preferred_element_type=jnp.float32), 1.0).astype(jnp.bfloat16)
    return reached


def local(queries, cache, draft_kv, out_weight, lengths, parents, path, accepted):
    s = lax.axis_index("seq")
    drafts = lax.all_gather(draft_kv, "seq", axis=1, tiled=True)
    o, st, new_cache = attend(lengths, queries, cache)
    m, l = st[:, 0, :], st[:, 1, :]
    reach = closure(lax.dynamic_index_in_dim(parents, s, 0, False))
    q = stacked_heads(lax.dynamic_slice_in_dim(queries, s * Q, Q, 0))
    ds = lax.dot_general(draft_kv[0], q, (((1,), (1,)), ((), ())), preferred_element_type=jnp.float32)
    ok = jnp.tile(reach.T, (1, q.shape[0] // Q)) > 0.5
    ds = jnp.where(ok, ds, DEAD)
    dm = jnp.max(ds, axis=0) * SCALE
    dp = jnp.where(ok, jnp.exp2(ds * SCALE - dm), 0.0)
    dl = jnp.sum(dp, axis=0)
    do = lax.dot_general(draft_kv[1], dp.astype(jnp.bfloat16), (((0,), (0,)), ((), ())), preferred_element_type=jnp.float32)
    mine = jnp.arange(m.shape[0]) == s
    top = lax.pmax(jnp.maximum(m, jnp.where(mine[:, None], dm[None], DEAD)), "seq")
    f = jnp.exp2(m - top)
    df = jnp.where(mine[:, None], jnp.exp2(dm[None] - top), 0.0)
    total = lax.psum(l * f + dl[None] * df, "seq")
    part = (o.astype(jnp.float32) * f[:, None, :] + do[None] * df[:, None, :]) / total[:, None, :]
    one = lax.psum_scatter(part, "seq", scatter_dimension=0, tiled=True)[0].astype(jnp.bfloat16)
    heads = one.shape[1] // Q
    one = one.reshape(HEAD, heads, Q).transpose(2, 1, 0).reshape(Q, heads * HEAD)
    attended = lax.all_gather(one, "seq", axis=0, tiled=True)
    attn_out = lax.psum_scatter(
        jnp.dot(attended, out_weight, preferred_element_type=jnp.float32), "tp", scatter_dimension=0, tiled=True
    ).astype(jnp.bfloat16)
    return attn_out, commit(lengths, path, accepted, drafts, new_cache)


def solution(mesh):
    return jax.shard_map(
        local,
        mesh=mesh,
        in_specs=(
            P(None, "tp"),
            P(None, None, "seq", "tp"),
            P(None, "seq", "tp"),
            P("tp", "seq"),
            P(),
            P(),
            P(),
            P(),
        ),
        out_specs=(P("tp", "seq"), P(None, None, "seq", "tp")),
        check_vma=False,
    )
```

```python
import functools

import jax
import jax.numpy as jnp
from jax import lax
from jax.experimental import pallas as pl
from jax.experimental.pallas import tpu as pltpu
from jax.sharding import PartitionSpec as P

HEAD = 128
Q = 64
ACC = 8
MESH = pl.DeviceIdType.MESH
SCALE = HEAD**-0.5 * 1.4426950408889634
DEAD = -1e30
CHUNK = 256
WINDOW = 32


def stacked_heads(rows):
    heads = rows.shape[1] // HEAD
    return jnp.concatenate([rows[:, h * HEAD : (h + 1) * HEAD] for h in range(heads)], axis=0)


def attend_kernel(len_ref, q_ref, kv_ref, o_ref, st_ref, nc_ref, s_ref, acc_ref, max_ref, sem):
    span = kv_ref.shape[2]
    chunks = span // CHUNK
    width = s_ref.shape[1]
    r = pl.program_id(0)
    live = jnp.clip(len_ref[r] - lax.axis_index("seq") * span, 0, span)
    copy = pltpu.make_async_copy(kv_ref, nc_ref.at[:, pl.ds(r, 1)], sem)
    copy.start()

    def scores(at):
        return lax.dot_general(
            kv_ref[0, 0, pl.ds(at, CHUNK), :],
            stacked_heads(q_ref[...]),
            (((1,), (1,)), ((), ())),
            preferred_element_type=jnp.float32,
        )

    def folded(s):
        return jnp.max(s.reshape(CHUNK // 8, 8, width), axis=0)

    def weighted(at, p):
        values = kv_ref[1, 0, pl.ds(at, CHUNK), :].T
        values = jnp.concatenate([values, jnp.ones((16, CHUNK), values.dtype)], axis=0)
        return jnp.dot(values, p, preferred_element_type=jnp.float32)

    def publish(peak, acc):
        o_ref[0] = acc[:HEAD].astype(o_ref.dtype)
        st_ref[0, 0:1] = peak
        st_ref[0, 1:2] = acc[HEAD : HEAD + 1]

    @pl.when(live == 0)
    def _():
        publish(jnp.full((1, width), DEAD, jnp.float32), jnp.zeros((HEAD + 16, width), jnp.float32))

    @pl.when(live == span)
    def _():
        peak = None
        for c in range(chunks):
            s = scores(c * CHUNK)
            s_ref[pl.ds(c * CHUNK, CHUNK), :] = s
            peak = folded(s) if peak is None else jnp.maximum(peak, folded(s))
        peak = jnp.max(peak, axis=0, keepdims=True) * SCALE
        acc = None
        for c in range(chunks):
            p = jnp.exp2(s_ref[pl.ds(c * CHUNK, CHUNK), :] * SCALE - peak).astype(jnp.bfloat16)
            term = weighted(c * CHUNK, p)
            acc = term if acc is None else acc + term
        publish(peak, acc)

    @pl.when((live > 0) & (live < span))
    def _():
        used = (live + CHUNK - 1) // CHUNK
        max_ref[...] = jnp.full_like(max_ref, DEAD)
        acc_ref[...] = jnp.zeros_like(acc_ref)

        def first(c, _):
            at = pl.multiple_of(c * CHUNK, CHUNK)
            row = lax.broadcasted_iota(jnp.int32, (CHUNK, width), 0) + at
            s = jnp.where(row < live, scores(at), DEAD)
            s_ref[pl.ds(at, CHUNK), :] = s
            max_ref[...] = jnp.maximum(max_ref[...], folded(s))
            return 0

        lax.fori_loop(0, used, first, 0)
        peak = jnp.max(max_ref[...], axis=0, keepdims=True) * SCALE

        def second(c, _):
            at = pl.multiple_of(c * CHUNK, CHUNK)
            row = lax.broadcasted_iota(jnp.int32, (CHUNK, width), 0) + at
            p = jnp.exp2(s_ref[pl.ds(at, CHUNK), :] * SCALE - peak)
            p = jnp.where(row < live, p, 0.0).astype(jnp.bfloat16)
            acc_ref[...] += weighted(at, p)
            return 0

        lax.fori_loop(0, used, second, 0)
        publish(peak, acc_ref[...])

    copy.wait()


def attend(lengths, queries, cache):
    requests, span = cache.shape[1], cache.shape[2]
    width = queries.shape[1] // HEAD * Q
    return pl.pallas_call(
        attend_kernel,
        out_shape=(
            jax.ShapeDtypeStruct((requests, HEAD, width), jnp.bfloat16),
            jax.ShapeDtypeStruct((requests, 8, width), jnp.float32),
            jax.ShapeDtypeStruct(cache.shape, cache.dtype),
        ),
        grid_spec=pltpu.PrefetchScalarGridSpec(
            num_scalar_prefetch=1,
            grid=(requests,),
            in_specs=[
                pl.BlockSpec((Q, queries.shape[1]), lambda r, n: (r, 0)),
                pl.BlockSpec((2, 1, span, HEAD), lambda r, n: (0, r, 0, 0)),
            ],
            out_specs=(
                pl.BlockSpec((1, HEAD, width), lambda r, n: (r, 0, 0)),
                pl.BlockSpec((1, 8, width), lambda r, n: (r, 0, 0)),
                pl.BlockSpec(memory_space=pl.ANY),
            ),
            scratch_shapes=[
                pltpu.VMEM((span, width), jnp.float32),
                pltpu.VMEM((HEAD + 16, width), jnp.float32),
                pltpu.VMEM((8, width), jnp.float32),
                pltpu.SemaphoreType.DMA,
            ],
        ),
        compiler_params=pltpu.CompilerParams(vmem_limit_bytes=56 << 20),
        name="attend",
    )(lengths, queries, cache)


def commit_kernel(
    len_ref, path_ref, acc_ref, draft_ref, attn_ref, nc_in, out_ref, nc_ref, win_ref, load_sem, store_sem
):
    requests, span = nc_ref.shape[1], nc_ref.shape[2]
    base = lax.axis_index("seq") * span

    def place(r):
        off = len_ref[r] - base
        hit = (off + acc_ref[r] > 0) & (off < span)
        start = pl.multiple_of(jnp.clip(off // 16 * 16, 0, span - WINDOW), 16)
        return off, hit, start

    def load(r, start):
        return pltpu.make_async_copy(
            nc_ref.at[:, r, pl.ds(start, WINDOW), :], win_ref.at[r], load_sem.at[r]
        )

    def store(r, start):
        return pltpu.make_async_copy(
            win_ref.at[r], nc_ref.at[:, r, pl.ds(start, WINDOW), :], store_sem.at[r]
        )

    def begin(r, _):
        off, hit, start = place(r)

        @pl.when(hit)
        def _():
            load(r, start).start()

        return 0

    def change(r, _):
        off, hit, start = place(r)

        @pl.when(hit)
        def _():
            row = lax.broadcasted_iota(jnp.int32, (WINDOW, Q), 0) + (start - off)
            node = lax.broadcasted_iota(jnp.int32, (WINDOW, Q), 1)
            pick = jnp.zeros((WINDOW, Q), jnp.float32)
            for j in range(ACC):
                pick = jnp.where((row == j) & (node == path_ref[r, j]), 1.0, pick)
            slot = lax.broadcasted_iota(jnp.int32, (WINDOW, HEAD), 0) + (start - off)
            fresh = (slot >= 0) & (slot < acc_ref[r])
            load(r, start).wait()
            for x in range(2):
                rows = jnp.dot(
                    pick.astype(jnp.bfloat16),
                    draft_ref[x, pl.ds(pl.multiple_of(r * Q, Q), Q), :],
                    preferred_element_type=jnp.float32,
                )
                old = win_ref[r, x].astype(jnp.float32)
                win_ref[r, x] = jnp.where(fresh, rows, old).astype(jnp.bfloat16)
            store(r, start).start()

        return 0

    def end(r, _):
        off, hit, start = place(r)

        @pl.when(hit)
        def _():
            store(r, start).wait()

        return 0

    lax.fori_loop(0, requests, begin, 0)
    out_ref[...] = attn_ref[...]
    lax.fori_loop(0, requests, change, 0)
    lax.fori_loop(0, requests, end, 0)


def commit(lengths, path, accepted, drafts, attn, new_cache):
    requests = new_cache.shape[1]
    return pl.pallas_call(
        commit_kernel,
        out_shape=(
            jax.ShapeDtypeStruct(attn.shape, attn.dtype),
            jax.ShapeDtypeStruct(new_cache.shape, new_cache.dtype),
        ),
        in_specs=[pl.BlockSpec(memory_space=pltpu.SMEM)] * 3
        + [pl.BlockSpec(memory_space=pltpu.VMEM)] * 2
        + [pl.BlockSpec(memory_space=pl.ANY)],
        out_specs=(pl.BlockSpec(memory_space=pltpu.VMEM), pl.BlockSpec(memory_space=pl.ANY)),
        scratch_shapes=[
            pltpu.VMEM((requests, 2, WINDOW, HEAD), jnp.bfloat16),
            pltpu.SemaphoreType.DMA((requests,)),
            pltpu.SemaphoreType.DMA((requests,)),
        ],
        input_output_aliases={5: 1},
        name="commit",
    )(lengths, path, accepted, drafts, attn, new_cache)


def folded_parts(first, second):
    peak = jnp.maximum(first[0], second[0])
    a, b = jnp.exp2(first[0] - peak), jnp.exp2(second[0] - peak)
    return peak, first[1] * a + second[1] * b, a, b


def join_kernel(
    o_ref, st_ref, q_hbm, dkv_ref, par_ref, w_ref, out_ref,
    q_ref, pair_o, pair_st, merge_o, merge_st, acc_ref, run_ref, att, rs_send, rs_recv,
    q_sem, pair_ss, pair_rs, merge_ss, merge_rs, own_ss, relay_ss, pass_ss, att_rs, out_ss, out_rs,
):
    s, t = lax.axis_index("seq"), lax.axis_index("tp")
    k, c = s // 2, s % 2
    y, z = k // 4, k % 4
    chips, tps = pair_o.shape[0], rs_send.shape[0]
    partner = 2 * k + 1 - c
    width = o_ref.shape[2]
    heads = width // Q

    barrier = pltpu.get_barrier_semaphore()
    for d in range(1, chips):
        pl.semaphore_signal(barrier, inc=1, device_id={"seq": 2 * ((k + d) % chips) + c}, device_id_type=MESH)
    pl.semaphore_signal(barrier, inc=1, device_id={"seq": partner}, device_id_type=MESH)
    for d in range(1, tps):
        pl.semaphore_signal(barrier, inc=1, device_id={"tp": (t + d) % tps}, device_id_type=MESH)
    q_copy = pltpu.make_async_copy(q_hbm.at[pl.ds(pl.multiple_of(s * Q, Q), Q), :], q_ref, q_sem)
    q_copy.start()
    pl.semaphore_wait(barrier, chips + tps - 1)

    def send(src, dst, ss, rs, **where):
        return pltpu.make_async_remote_copy(
            src_ref=src, dst_ref=dst, send_sem=ss, recv_sem=rs, device_id=where, device_id_type=MESH
        )

    def pair_copies(j):
        r = 2 * j + 1 - c
        return (
            send(o_ref.at[r], pair_o.at[j], pair_ss.at[j, 0], pair_rs.at[j, 0], seq=partner),
            send(st_ref.at[r], pair_st.at[j], pair_ss.at[j, 1], pair_rs.at[j, 1], seq=partner),
        )

    def merge_copies(j):
        return (
            send(pair_o.at[j], merge_o.at[k], merge_ss.at[j, 0], merge_rs.at[k, 0], seq=2 * j + c),
            send(pair_st.at[j], merge_st.at[k], merge_ss.at[j, 1], merge_rs.at[k, 1], seq=2 * j + c),
        )

    def merge_arrival(i):
        return (
            send(pair_o.at[i], merge_o.at[i], merge_ss.at[i, 0], merge_rs.at[i, 0], seq=partner),
            send(pair_st.at[i], merge_st.at[i], merge_ss.at[i, 1], merge_rs.at[i, 1], seq=partner),
        )

    def pass_on(slot, ss, where):
        return send(att.at[slot], att.at[slot], ss, att_rs.at[slot], seq=where)

    def ring(d):
        return 2 * (y * 4 + (z + d) % 4) + c

    def out_copy(g):
        return send(rs_send.at[g], rs_recv.at[t], out_ss.at[g], out_rs.at[t], tp=g)

    def out_arrival(i):
        return send(rs_send.at[i], rs_recv.at[i], out_ss.at[i], out_rs.at[i], seq=partner)

    def reach_of(j, parity):
        return (1 + 3 * (j % 2)) * (1 + parity)

    def in_order(i):
        return (k // 2 * 2 + 2 * (i % 4) + i // 4) % chips

    def start_pair(i, _):
        j = in_order(i)

        @pl.when(k < reach_of(j, 1 - c))
        def _():
            for copy in pair_copies(j):
                copy.start()

        return 0

    lax.fori_loop(0, chips, start_pair, 0)

    node = lax.broadcasted_iota(jnp.int32, (Q, Q), 0)
    other = lax.broadcasted_iota(jnp.int32, (Q, Q), 1)
    parent = jnp.broadcast_to(par_ref[pl.ds(s, 1), :], (Q, Q))
    reach = jnp.where((node == other) | (node == parent), 1.0, 0.0)
    for _ in range((Q - 1).bit_length()):
        bits = reach.astype(jnp.bfloat16)
        reach = jnp.minimum(jnp.dot(bits, bits, preferred_element_type=jnp.float32), 1.0)
    lane = lax.broadcasted_iota(jnp.int32, (Q, width), 1) % Q
    spread = jnp.where(lane == lax.broadcasted_iota(jnp.int32, (Q, width), 0), 1.0, 0.0).astype(jnp.bfloat16)
    alive = jnp.dot(reach.astype(jnp.bfloat16), spread, preferred_element_type=jnp.float32) > 0.5
    q_copy.wait()
    scores = lax.dot_general(
        dkv_ref[0], stacked_heads(q_ref[...]), (((1,), (1,)), ((), ())), preferred_element_type=jnp.float32
    )
    scores = jnp.where(alive, scores, DEAD)
    peak = jnp.max(scores, axis=0, keepdims=True) * SCALE
    weights = jnp.where(alive, jnp.exp2(scores * SCALE - peak), 0.0)
    run_ref[0:1] = peak
    run_ref[1:2] = jnp.sum(weights, axis=0, keepdims=True)
    acc_ref[...] = jnp.dot(dkv_ref[1].T, weights.astype(jnp.bfloat16), preferred_element_type=jnp.float32)

    def combine(i, _):
        j = in_order(i)
        r = 2 * j + c

        @pl.when(k < reach_of(j, c))
        def _():
            for copy in pair_copies(j):
                copy.wait_recv()
            peak, total, a, b = folded_parts(
                (st_ref[r, 0:1], st_ref[r, 1:2]), (pair_st[j, 0:1], pair_st[j, 1:2])
            )
            mixed = o_ref[r].astype(jnp.float32) * a + pair_o[j].astype(jnp.float32) * b
            pair_o[j] = mixed.astype(jnp.bfloat16)
            pair_st[j, 0:1] = peak
            pair_st[j, 1:2] = total

            @pl.when(j != k)
            def _():
                for copy in merge_copies(j):
                    copy.start()

        return 0

    lax.fori_loop(0, chips, combine, 0)

    def absorb(o, st):
        peak, total, a, b = folded_parts((run_ref[0:1], run_ref[1:2]), (st[0:1], st[1:2]))
        acc_ref[...] = acc_ref[...] * a + o[...].astype(jnp.float32) * b
        run_ref[0:1] = peak
        run_ref[1:2] = total

    def merge(i, _):
        j = (k + i) % chips

        @pl.when(j < reach_of(k, c))
        def _():
            @pl.when(j == k)
            def _():
                absorb(pair_o.at[j], pair_st.at[j])

            @pl.when(j != k)
            def _():
                for copy in merge_arrival(j):
                    copy.wait_recv()
                absorb(merge_o.at[j], merge_st.at[j])

        return 0

    lax.fori_loop(0, chips, merge, 0)

    done = (acc_ref[...] / run_ref[1:2]).T.astype(jnp.bfloat16)
    for h in range(heads):
        att[s, :, h * HEAD : (h + 1) * HEAD] = done[h * Q : (h + 1) * Q]

    twin = (k + 4) % chips
    own = [pass_on(s, own_ss.at[0], 2 * twin + c)]
    own += [pass_on(s, own_ss.at[d], ring(d)) for d in (1, 3, 2)]
    own += [pass_on(s, own_ss.at[4], partner)]
    for copy in own:
        copy.start()

    def group(i):
        return (y + i // 2) % 2 * 4 + (z // 2 * 2 + 2 * i + i // 4) % 4

    def forward(g):
        return pass_on(2 * g + c, pass_ss.at[g], partner)

    def relays():
        return [pass_on(2 * twin + c, relay_ss.at[d], ring(d)) for d in (1, 3, 2)]

    def arrival(slot):
        return pass_on(slot, own_ss.at[0], partner)

    def project(g):
        arrival(2 * g + 1 - c).wait_recv()
        rows = att[pl.ds(2 * g, 2)].reshape(2 * Q, att.shape[2])
        rs_send[g] = jnp.dot(rows, w_ref[...], preferred_element_type=jnp.float32).astype(jnp.bfloat16)

        @pl.when(g != t)
        def _():
            out_copy(g).start()

    def spread_on(i, _):
        g = group(i)

        @pl.when(g != k)
        def _():
            arrival(2 * g + c).wait_recv()
            forward(g).start()

        @pl.when(g == twin)
        def _():
            for copy in relays():
                copy.start()

        @pl.when(i > 0)
        def _():
            project(group(i - 1))

        return 0

    lax.fori_loop(0, chips, spread_on, 0)
    project(group(chips - 1))

    total = rs_send[t].astype(jnp.float32)
    for d in range(1, tps):
        i = (t + d) % tps
        out_arrival(i).wait_recv()
        total = total + rs_recv[i].astype(jnp.float32)
    out_ref[...] = total.astype(out_ref.dtype)

    def finish_pair(j, _):
        @pl.when(k < reach_of(j, 1 - c))
        def _():
            for copy in pair_copies(j):
                copy.wait_send()

        @pl.when((k < reach_of(j, c)) & (j != k))
        def _():
            for copy in merge_copies(j):
                copy.wait_send()

        @pl.when(j != k)
        def _():
            forward(j).wait_send()

        @pl.when(j != t)
        def _():
            out_copy(j).wait_send()

        return 0

    lax.fori_loop(0, chips, finish_pair, 0)
    for copy in own + relays():
        copy.wait_send()


def join(o, st, queries, draft_kv, parents, out_weight, chips, tps):
    requests, _, width = o.shape
    wide, columns = queries.shape[1], out_weight.shape[1]
    dma = pltpu.SemaphoreType.DMA
    whole = pl.BlockSpec(memory_space=pltpu.VMEM)
    return pl.pallas_call(
        join_kernel,
        out_shape=jax.ShapeDtypeStruct((queries.shape[0] // tps, columns), jnp.bfloat16),
        in_specs=[whole, whole, pl.BlockSpec(memory_space=pl.ANY), whole, whole, whole],
        out_specs=whole,
        scratch_shapes=[
            pltpu.VMEM((Q, wide), jnp.bfloat16),
            pltpu.VMEM((chips, HEAD, width), jnp.bfloat16),
            pltpu.VMEM((chips, 8, width), jnp.float32),
            pltpu.VMEM((chips, HEAD, width), jnp.bfloat16),
            pltpu.VMEM((chips, 8, width), jnp.float32),
            pltpu.VMEM((HEAD, width), jnp.float32),
            pltpu.VMEM((8, width), jnp.float32),
            pltpu.VMEM((requests, Q, wide), jnp.bfloat16),
            pltpu.VMEM((tps, 2 * Q, columns), jnp.bfloat16),
            pltpu.VMEM((tps, 2 * Q, columns), jnp.bfloat16),
            dma,
            dma((chips, 2)),
            dma((chips, 2)),
            dma((chips, 2)),
            dma((chips, 2)),
            dma((5,)),
            dma((4,)),
            dma((chips,)),
            dma((requests,)),
            dma((tps,)),
            dma((tps,)),
        ],
        compiler_params=pltpu.CompilerParams(
            collective_id=0, has_side_effects=True, vmem_limit_bytes=40 << 20
        ),
        name="join",
    )(o, st, queries, draft_kv, parents, out_weight)


def solution(mesh):
    chips, tps = mesh.shape["seq"] // 2, mesh.shape["tp"]

    def local(queries, cache, draft_kv, out_weight, lengths, parents, path, accepted):
        drafts = lax.all_gather(draft_kv, "seq", axis=1, tiled=True)
        o, st, new_cache = attend(lengths, queries, cache)
        attn = join(o, st, queries, draft_kv, parents, out_weight, chips, tps)
        return commit(lengths, path, accepted, drafts, attn, new_cache)

    return jax.shard_map(
        local,
        mesh=mesh,
        in_specs=(
            P(None, "tp"),
            P(None, None, "seq", "tp"),
            P(None, "seq", "tp"),
            P("tp", "seq"),
            P(),
            P(),
            P(),
            P(),
        ),
        out_specs=(P("tp", "seq"), P(None, None, "seq", "tp")),
        check_vma=False,
    )
```

```python
import functools

import jax
import jax.numpy as jnp
from jax import lax
from jax.experimental import pallas as pl
from jax.experimental.pallas import tpu as pltpu
from jax.sharding import PartitionSpec as P

HEAD = 128
Q = 64
ACC = 8
MESH = pl.DeviceIdType.MESH
SCALE = HEAD**-0.5 * 1.4426950408889634
DEAD = -1e30
CHUNK = 256
WINDOW = 32


def stacked_heads(rows):
    heads = rows.shape[1] // HEAD
    return jnp.concatenate([rows[:, h * HEAD : (h + 1) * HEAD] for h in range(heads)], axis=0)


def attend_kernel(
    len_ref, q_hbm, kv_hbm, o_ref, st_ref, nc_ref, q_ref, kv_ref, s_ref, acc_ref, max_ref, q_sem, load_sem, store_sem
):
    requests, span = kv_ref.shape[0], kv_ref.shape[2]
    chunks = span // CHUNK
    width = s_ref.shape[1]
    base = lax.axis_index("seq") * span

    def q_load(r):
        rows = pl.ds(pl.multiple_of(r * Q, Q), Q)
        return pltpu.make_async_copy(q_hbm.at[rows, :], q_ref.at[r], q_sem.at[r])

    def load(r):
        return pltpu.make_async_copy(kv_hbm.at[:, r], kv_ref.at[r], load_sem.at[r])

    def store(r):
        return pltpu.make_async_copy(kv_ref.at[r], nc_ref.at[:, r], store_sem.at[r])

    def begin(r, _):
        q_load(r).start()
        load(r).start()
        return 0

    lax.fori_loop(0, requests, begin, 0)

    def one(r, _):
        live = jnp.clip(len_ref[r] - base, 0, span)
        q_load(r).wait()
        load(r).wait()
        store(r).start()

        def scores(at):
            return lax.dot_general(
                kv_ref[r, 0, pl.ds(at, CHUNK), :],
                stacked_heads(q_ref[r]),
                (((1,), (1,)), ((), ())),
                preferred_element_type=jnp.float32,
            )

        def folded(s):
            return jnp.max(s.reshape(CHUNK // 8, 8, width), axis=0)

        def weighted(at, p):
            values = kv_ref[r, 1, pl.ds(at, CHUNK), :].T
            values = jnp.concatenate([values, jnp.ones((16, CHUNK), values.dtype)], axis=0)
            return jnp.dot(values, p, preferred_element_type=jnp.float32)

        def publish(peak, acc):
            o_ref[r] = acc[:HEAD].astype(o_ref.dtype)
            st_ref[r, 0:1] = peak
            st_ref[r, 1:2] = acc[HEAD : HEAD + 1]

        @pl.when(live == 0)
        def _():
            publish(jnp.full((1, width), DEAD, jnp.float32), jnp.zeros((HEAD + 16, width), jnp.float32))

        @pl.when(live == span)
        def _():
            peak = None
            for c in range(chunks):
                s = scores(c * CHUNK)
                s_ref[pl.ds(c * CHUNK, CHUNK), :] = s
                peak = folded(s) if peak is None else jnp.maximum(peak, folded(s))
            peak = jnp.max(peak, axis=0, keepdims=True) * SCALE
            acc = None
            for c in range(chunks):
                p = jnp.exp2(s_ref[pl.ds(c * CHUNK, CHUNK), :] * SCALE - peak).astype(jnp.bfloat16)
                term = weighted(c * CHUNK, p)
                acc = term if acc is None else acc + term
            publish(peak, acc)

        @pl.when((live > 0) & (live < span))
        def _():
            used = (live + CHUNK - 1) // CHUNK
            max_ref[...] = jnp.full_like(max_ref, DEAD)
            acc_ref[...] = jnp.zeros_like(acc_ref)

            def first(c, _):
                at = pl.multiple_of(c * CHUNK, CHUNK)
                row = lax.broadcasted_iota(jnp.int32, (CHUNK, width), 0) + at
                s = jnp.where(row < live, scores(at), DEAD)
                s_ref[pl.ds(at, CHUNK), :] = s
                max_ref[...] = jnp.maximum(max_ref[...], folded(s))
                return 0

            lax.fori_loop(0, used, first, 0)
            peak = jnp.max(max_ref[...], axis=0, keepdims=True) * SCALE

            def second(c, _):
                at = pl.multiple_of(c * CHUNK, CHUNK)
                row = lax.broadcasted_iota(jnp.int32, (CHUNK, width), 0) + at
                p = jnp.exp2(s_ref[pl.ds(at, CHUNK), :] * SCALE - peak)
                p = jnp.where(row < live, p, 0.0).astype(jnp.bfloat16)
                acc_ref[...] += weighted(at, p)
                return 0

            lax.fori_loop(0, used, second, 0)
            publish(peak, acc_ref[...])

        return 0

    lax.fori_loop(0, requests, one, 0)

    def end(r, _):
        store(r).wait()
        return 0

    lax.fori_loop(0, requests, end, 0)


def attend(lengths, queries, cache):
    requests, span = cache.shape[1], cache.shape[2]
    wide = queries.shape[1]
    width = wide // HEAD * Q
    return pl.pallas_call(
        attend_kernel,
        out_shape=(
            jax.ShapeDtypeStruct((requests, HEAD, width), jnp.bfloat16),
            jax.ShapeDtypeStruct((requests, 8, width), jnp.float32),
            jax.ShapeDtypeStruct(cache.shape, cache.dtype),
        ),
        in_specs=[
            pl.BlockSpec(memory_space=pltpu.SMEM),
            pl.BlockSpec(memory_space=pltpu.HBM),
            pl.BlockSpec(memory_space=pltpu.HBM),
        ],
        out_specs=(
            pl.BlockSpec(memory_space=pltpu.VMEM),
            pl.BlockSpec(memory_space=pltpu.VMEM),
            pl.BlockSpec(memory_space=pltpu.HBM),
        ),
        scratch_shapes=[
            pltpu.VMEM((requests, Q, wide), jnp.bfloat16),
            pltpu.VMEM((requests, 2, span, HEAD), jnp.bfloat16),
            pltpu.VMEM((span, width), jnp.float32),
            pltpu.VMEM((HEAD + 16, width), jnp.float32),
            pltpu.VMEM((8, width), jnp.float32),
            pltpu.SemaphoreType.DMA((requests,)),
            pltpu.SemaphoreType.DMA((requests,)),
            pltpu.SemaphoreType.DMA((requests,)),
        ],
        compiler_params=pltpu.CompilerParams(vmem_limit_bytes=60 << 20),
        name="attend",
    )(lengths, queries, cache)


def commit_kernel(
    len_ref, acc_ref, chosen_ref, attn_ref, nc_in, out_ref, nc_ref, win_ref, load_sem, store_sem
):
    requests, span = nc_ref.shape[1], nc_ref.shape[2]
    base = lax.axis_index("seq") * span

    def place(r):
        off = len_ref[r] - base
        hit = (off + acc_ref[r] > 0) & (off < span)
        start = pl.multiple_of(jnp.clip(off // 16 * 16, 0, span - WINDOW), 16)
        return off, hit, start

    def load(r, start):
        return pltpu.make_async_copy(
            nc_ref.at[:, r, pl.ds(start, WINDOW), :], win_ref.at[r], load_sem.at[r]
        )

    def store(r, start):
        return pltpu.make_async_copy(
            win_ref.at[r], nc_ref.at[:, r, pl.ds(start, WINDOW), :], store_sem.at[r]
        )

    def begin(r, _):
        off, hit, start = place(r)

        @pl.when(hit)
        def _():
            load(r, start).start()

        return 0

    def change(r, _):
        off, hit, start = place(r)

        @pl.when(hit)
        def _():
            row = lax.broadcasted_iota(jnp.int32, (WINDOW, 2 * ACC), 0) + (start - off)
            node = lax.broadcasted_iota(jnp.int32, (WINDOW, 2 * ACC), 1)
            pick = jnp.where(row == node, 1.0, 0.0).astype(jnp.bfloat16)
            slot = lax.broadcasted_iota(jnp.int32, (WINDOW, HEAD), 0) + (start - off)
            fresh = (slot >= 0) & (slot < acc_ref[r])
            load(r, start).wait()
            for x in range(2):
                rows = jnp.dot(
                    pick,
                    chosen_ref[r, 2 * ACC * x : 2 * ACC * (x + 1)],
                    preferred_element_type=jnp.float32,
                )
                old = win_ref[r, x].astype(jnp.float32)
                win_ref[r, x] = jnp.where(fresh, rows, old).astype(jnp.bfloat16)
            store(r, start).start()

        return 0

    def end(r, _):
        off, hit, start = place(r)

        @pl.when(hit)
        def _():
            store(r, start).wait()

        return 0

    lax.fori_loop(0, requests, begin, 0)
    out_ref[...] = attn_ref[...]
    lax.fori_loop(0, requests, change, 0)
    lax.fori_loop(0, requests, end, 0)


def commit(lengths, accepted, chosen, attn, new_cache):
    requests = new_cache.shape[1]
    return pl.pallas_call(
        commit_kernel,
        out_shape=(
            jax.ShapeDtypeStruct(attn.shape, attn.dtype),
            jax.ShapeDtypeStruct(new_cache.shape, new_cache.dtype),
        ),
        in_specs=[pl.BlockSpec(memory_space=pltpu.SMEM)] * 2
        + [pl.BlockSpec(memory_space=pltpu.VMEM)] * 2
        + [pl.BlockSpec(memory_space=pl.ANY)],
        out_specs=(pl.BlockSpec(memory_space=pltpu.VMEM), pl.BlockSpec(memory_space=pl.ANY)),
        scratch_shapes=[
            pltpu.VMEM((requests, 2, WINDOW, HEAD), jnp.bfloat16),
            pltpu.SemaphoreType.DMA((requests,)),
            pltpu.SemaphoreType.DMA((requests,)),
        ],
        input_output_aliases={4: 1},
        name="commit",
    )(lengths, accepted, chosen, attn, new_cache)


def folded_parts(first, second):
    peak = jnp.maximum(first[0], second[0])
    a, b = jnp.exp2(first[0] - peak), jnp.exp2(second[0] - peak)
    return peak, first[1] * a + second[1] * b, a, b


def join_kernel(
    o_hbm, st_hbm, q_hbm, dkv_ref, par_ref, path_ref, w_hbm, out_ref, chosen_ref,
    q_ref, o_ref, st_ref, w_ref, pair_o, pair_st, merge_o, merge_st, acc_ref, run_ref, att, rs_send, rs_recv,
    q_sem, in_sem, pair_ss, pair_rs, merge_ss, merge_rs, own_ss, relay_ss, pass_ss, att_rs, out_ss, out_rs,
):
    s, t = lax.axis_index("seq"), lax.axis_index("tp")
    k, c = s // 2, s % 2
    y, z = k // 4, k % 4
    chips, tps = pair_o.shape[0], rs_send.shape[0]
    partner = 2 * k + 1 - c
    width = o_ref.shape[2]
    heads = width // Q

    barrier = pltpu.get_barrier_semaphore()
    for d in range(1, chips):
        pl.semaphore_signal(barrier, inc=1, device_id={"seq": 2 * ((k + d) % chips) + c}, device_id_type=MESH)
    pl.semaphore_signal(barrier, inc=1, device_id={"seq": partner}, device_id_type=MESH)
    for d in range(1, tps):
        pl.semaphore_signal(barrier, inc=1, device_id={"tp": (t + d) % tps}, device_id_type=MESH)
    q_copy = pltpu.make_async_copy(q_hbm.at[pl.ds(pl.multiple_of(s * Q, Q), Q), :], q_ref, q_sem)
    q_copy.start()
    w_copy = pltpu.make_async_copy(w_hbm, w_ref, in_sem.at[0])
    o_copy = pltpu.make_async_copy(o_hbm, o_ref, in_sem.at[1])
    st_copy = pltpu.make_async_copy(st_hbm, st_ref, in_sem.at[2])
    for copy in (o_copy, st_copy, w_copy):
        copy.start()
    o_copy.wait()
    st_copy.wait()
    pl.semaphore_wait(barrier, chips + tps - 1)

    def send(src, dst, ss, rs, **where):
        return pltpu.make_async_remote_copy(
            src_ref=src, dst_ref=dst, send_sem=ss, recv_sem=rs, device_id=where, device_id_type=MESH
        )

    def pair_copies(j):
        r = 2 * j + 1 - c
        return (
            send(o_ref.at[r], pair_o.at[j], pair_ss.at[j, 0], pair_rs.at[j, 0], seq=partner),
            send(st_ref.at[r], pair_st.at[j], pair_ss.at[j, 1], pair_rs.at[j, 1], seq=partner),
        )

    def merge_copies(j):
        return (
            send(pair_o.at[j], merge_o.at[k], merge_ss.at[j, 0], merge_rs.at[k, 0], seq=2 * j + c),
            send(pair_st.at[j], merge_st.at[k], merge_ss.at[j, 1], merge_rs.at[k, 1], seq=2 * j + c),
        )

    def merge_arrival(i):
        return (
            send(pair_o.at[i], merge_o.at[i], merge_ss.at[i, 0], merge_rs.at[i, 0], seq=partner),
            send(pair_st.at[i], merge_st.at[i], merge_ss.at[i, 1], merge_rs.at[i, 1], seq=partner),
        )

    def pass_on(slot, ss, where):
        return send(att.at[slot], att.at[slot], ss, att_rs.at[slot], seq=where)

    def ring(d):
        return 2 * (y * 4 + (z + d) % 4) + c

    def out_copy(g):
        return send(rs_send.at[g], rs_recv.at[t], out_ss.at[g], out_rs.at[t], tp=g)

    def out_arrival(i):
        return send(rs_send.at[i], rs_recv.at[i], out_ss.at[i], out_rs.at[i], seq=partner)

    def reach_of(j, parity):
        return (1 + 3 * (j % 2)) * (1 + parity)

    def in_order(i):
        return (k // 2 * 2 + 2 * (i % 4) + i // 4) % chips

    def start_pair(i, _):
        j = in_order(i)

        @pl.when(k < reach_of(j, 1 - c))
        def _():
            for copy in pair_copies(j):
                copy.start()

        return 0

    lax.fori_loop(0, chips, start_pair, 0)

    node = lax.broadcasted_iota(jnp.int32, (Q, Q), 0)
    other = lax.broadcasted_iota(jnp.int32, (Q, Q), 1)
    parent = jnp.broadcast_to(par_ref[pl.ds(s, 1), :], (Q, Q))
    reach = jnp.where((node == other) | (node == parent), 1.0, 0.0)
    for _ in range((Q - 1).bit_length()):
        bits = reach.astype(jnp.bfloat16)
        reach = jnp.minimum(jnp.dot(bits, bits, preferred_element_type=jnp.float32), 1.0)
    lane = lax.broadcasted_iota(jnp.int32, (Q, width), 1) % Q
    spread = jnp.where(lane == lax.broadcasted_iota(jnp.int32, (Q, width), 0), 1.0, 0.0).astype(jnp.bfloat16)
    alive = jnp.dot(reach.astype(jnp.bfloat16), spread, preferred_element_type=jnp.float32) > 0.5
    q_copy.wait()
    scores = lax.dot_general(
        dkv_ref[0], stacked_heads(q_ref[...]), (((1,), (1,)), ((), ())), preferred_element_type=jnp.float32
    )
    scores = jnp.where(alive, scores, DEAD)
    peak = jnp.max(scores, axis=0, keepdims=True) * SCALE
    weights = jnp.where(alive, jnp.exp2(scores * SCALE - peak), 0.0)
    run_ref[0:1] = peak
    run_ref[1:2] = jnp.sum(weights, axis=0, keepdims=True)
    acc_ref[...] = jnp.dot(dkv_ref[1].T, weights.astype(jnp.bfloat16), preferred_element_type=jnp.float32)

    def combine(i, _):
        j = in_order(i)
        r = 2 * j + c

        @pl.when(k < reach_of(j, c))
        def _():
            for copy in pair_copies(j):
                copy.wait_recv()
            peak, total, a, b = folded_parts(
                (st_ref[r, 0:1], st_ref[r, 1:2]), (pair_st[j, 0:1], pair_st[j, 1:2])
            )
            mixed = o_ref[r].astype(jnp.float32) * a + pair_o[j].astype(jnp.float32) * b
            pair_o[j] = mixed.astype(jnp.bfloat16)
            pair_st[j, 0:1] = peak
            pair_st[j, 1:2] = total

            @pl.when(j != k)
            def _():
                for copy in merge_copies(j):
                    copy.start()

        return 0

    lax.fori_loop(0, chips, combine, 0)

    def absorb(o, st):
        peak, total, a, b = folded_parts((run_ref[0:1], run_ref[1:2]), (st[0:1], st[1:2]))
        acc_ref[...] = acc_ref[...] * a + o[...].astype(jnp.float32) * b
        run_ref[0:1] = peak
        run_ref[1:2] = total

    def merge(i, _):
        j = (k + i) % chips

        @pl.when(j < reach_of(k, c))
        def _():
            @pl.when(j == k)
            def _():
                absorb(pair_o.at[j], pair_st.at[j])

            @pl.when(j != k)
            def _():
                for copy in merge_arrival(j):
                    copy.wait_recv()
                absorb(merge_o.at[j], merge_st.at[j])

        return 0

    lax.fori_loop(0, chips, merge, 0)

    att[s, :width] = (acc_ref[...] / run_ref[1:2]).T.astype(jnp.bfloat16)
    lanes = lax.broadcasted_iota(jnp.int32, path_ref.shape, 1)
    nodes = jnp.sum(jnp.where(lanes == s, path_ref[...], 0), axis=1, keepdims=True)
    pick = jnp.where(lax.broadcasted_iota(jnp.int32, (ACC, Q), 1) == nodes, 1.0, 0.0)
    pick = jnp.concatenate([pick, jnp.zeros((ACC, Q), jnp.float32)], axis=0).astype(jnp.bfloat16)
    for x in range(2):
        rows = jnp.dot(pick, dkv_ref[x], preferred_element_type=jnp.float32)
        att[s, width + 2 * ACC * x : width + 2 * ACC * (x + 1)] = rows.astype(jnp.bfloat16)

    twin = (k + 4) % chips
    own = [pass_on(s, own_ss.at[0], 2 * twin + c)]
    own += [pass_on(s, own_ss.at[d], ring(d)) for d in (1, 3, 2)]
    own += [pass_on(s, own_ss.at[4], partner)]
    for copy in own:
        copy.start()

    def group(i):
        return (y + i // 2) % 2 * 4 + (z // 2 * 2 + 2 * i + i // 4) % 4

    def forward(g):
        return pass_on(2 * g + c, pass_ss.at[g], partner)

    def relays():
        return [pass_on(2 * twin + c, relay_ss.at[d], ring(d)) for d in (1, 3, 2)]

    def arrival(slot):
        return pass_on(slot, own_ss.at[0], partner)

    def project(g):
        arrival(2 * g + 1 - c).wait_recv()
        rows = jnp.concatenate(
            [
                jnp.concatenate([att[2 * g, h * Q : (h + 1) * Q], att[2 * g + 1, h * Q : (h + 1) * Q]], axis=0)
                for h in range(heads)
            ],
            axis=1,
        )
        rs_send[g] = jnp.dot(rows, w_ref[...], preferred_element_type=jnp.float32).astype(jnp.bfloat16)

        @pl.when(g != t)
        def _():
            out_copy(g).start()

    def spread_on(i, _):
        g = group(i)

        @pl.when(g != k)
        def _():
            arrival(2 * g + c).wait_recv()
            forward(g).start()

        @pl.when(g == twin)
        def _():
            for copy in relays():
                copy.start()

        @pl.when(i > 0)
        def _():
            project(group(i - 1))

        return 0

    w_copy.wait()
    lax.fori_loop(0, chips, spread_on, 0)
    project(group(chips - 1))

    total = rs_send[t].astype(jnp.float32)
    for d in range(1, tps):
        i = (t + d) % tps
        out_arrival(i).wait_recv()
        total = total + rs_recv[i].astype(jnp.float32)
    out_ref[...] = total.astype(out_ref.dtype)
    chosen_ref[...] = att[:, width:]

    def finish_pair(j, _):
        @pl.when(k < reach_of(j, 1 - c))
        def _():
            for copy in pair_copies(j):
                copy.wait_send()

        @pl.when((k < reach_of(j, c)) & (j != k))
        def _():
            for copy in merge_copies(j):
                copy.wait_send()

        @pl.when(j != k)
        def _():
            forward(j).wait_send()

        @pl.when(j != t)
        def _():
            out_copy(j).wait_send()

        return 0

    lax.fori_loop(0, chips, finish_pair, 0)
    for copy in own + relays():
        copy.wait_send()


def join(o, st, queries, draft_kv, parents, path, out_weight, chips, tps):
    requests, _, width = o.shape
    wide, columns = queries.shape[1], out_weight.shape[1]
    dma = pltpu.SemaphoreType.DMA
    whole, far = pl.BlockSpec(memory_space=pltpu.VMEM), pl.BlockSpec(memory_space=pl.ANY)
    return pl.pallas_call(
        join_kernel,
        out_shape=(
            jax.ShapeDtypeStruct((queries.shape[0] // tps, columns), jnp.bfloat16),
            jax.ShapeDtypeStruct((requests, 4 * ACC, HEAD), jnp.bfloat16),
        ),
        in_specs=[far, far, far, whole, whole, whole, far],
        out_specs=(whole, whole),
        scratch_shapes=[
            pltpu.VMEM((Q, wide), jnp.bfloat16),
            pltpu.VMEM(o.shape, o.dtype),
            pltpu.VMEM(st.shape, st.dtype),
            pltpu.VMEM(out_weight.shape, out_weight.dtype),
            pltpu.VMEM((chips, HEAD, width), jnp.bfloat16),
            pltpu.VMEM((chips, 8, width), jnp.float32),
            pltpu.VMEM((chips, HEAD, width), jnp.bfloat16),
            pltpu.VMEM((chips, 8, width), jnp.float32),
            pltpu.VMEM((HEAD, width), jnp.float32),
            pltpu.VMEM((8, width), jnp.float32),
            pltpu.VMEM((requests, width + 4 * ACC, HEAD), jnp.bfloat16),
            pltpu.VMEM((tps, 2 * Q, columns), jnp.bfloat16),
            pltpu.VMEM((tps, 2 * Q, columns), jnp.bfloat16),
            dma,
            dma((3,)),
            dma((chips, 2)),
            dma((chips, 2)),
            dma((chips, 2)),
            dma((chips, 2)),
            dma((5,)),
            dma((4,)),
            dma((chips,)),
            dma((requests,)),
            dma((tps,)),
            dma((tps,)),
        ],
        compiler_params=pltpu.CompilerParams(
            collective_id=0, has_side_effects=True, vmem_limit_bytes=60 << 20
        ),
        name="join",
    )(o, st, queries, draft_kv, parents, path, out_weight)


def solution(mesh):
    chips, tps = mesh.shape["seq"] // 2, mesh.shape["tp"]

    def local(queries, cache, draft_kv, out_weight, lengths, parents, path, accepted):
        o, st, new_cache = attend(lengths, queries, cache)
        attn, chosen = join(o, st, queries, draft_kv, parents, path.T, out_weight, chips, tps)
        return commit(lengths, accepted, chosen, attn, new_cache)

    return jax.shard_map(
        local,
        mesh=mesh,
        in_specs=(
            P(None, "tp"),
            P(None, None, "seq", "tp"),
            P(None, "seq", "tp"),
            P("tp", "seq"),
            P(),
            P(),
            P(),
            P(),
        ),
        out_specs=(P("tp", "seq"), P(None, None, "seq", "tp")),
        check_vma=False,
    )
```

```python
import functools

import jax
import jax.numpy as jnp
from jax import lax
from jax.experimental import pallas as pl
from jax.experimental.pallas import tpu as pltpu
from jax.sharding import PartitionSpec as P

HEAD = 128
Q = 64
ACC = 8
MESH = pl.DeviceIdType.MESH
SCALE = HEAD**-0.5 * 1.4426950408889634
DEAD = -1e30
CHUNK = 256
WINDOW = 32


def stacked_heads(rows):
    heads = rows.shape[1] // HEAD
    return jnp.concatenate([rows[:, h * HEAD : (h + 1) * HEAD] for h in range(heads)], axis=0)


def score_chunk(kv, q, c, live):
    s = lax.dot_general(
        kv[0, c * CHUNK : (c + 1) * CHUNK, :], q, (((1,), (1,)), ((), ())), preferred_element_type=jnp.float32
    )
    row = lax.broadcasted_iota(jnp.int32, s.shape, 0) + c * CHUNK
    return jnp.where(row < live, s, DEAD)


def attention_step(now, s_now, peak_now, later, q_later, live, s_later):
    acc = peak = None
    for c in range(s_now.shape[0] // CHUNK):
        rows = slice(c * CHUNK, (c + 1) * CHUNK)
        if later is not None:
            s = score_chunk(later, q_later, c, live)
            s_later[rows, :] = s
            top = jnp.max(s.reshape(CHUNK // 8, 8, s.shape[1]), axis=0)
            peak = top if peak is None else jnp.maximum(peak, top)
        if now is not None:
            p = jnp.exp2(s_now[rows, :] * SCALE - peak_now).astype(jnp.bfloat16)
            values = now[1, rows, :].T
            values = jnp.concatenate([values, jnp.ones((16, CHUNK), values.dtype)], axis=0)
            term = jnp.dot(values, p, preferred_element_type=jnp.float32)
            acc = term if acc is None else acc + term
    if peak is not None:
        peak = jnp.max(peak, axis=0, keepdims=True) * SCALE
    return acc, peak


def publish(o, st, peak, acc):
    o[...] = acc[:HEAD].astype(o.dtype)
    st[0:1] = peak
    st[1:2] = acc[HEAD : HEAD + 1]


def attend_kernel(
    len_ref, q_hbm, kv_hbm, o_hbm, st_hbm, nc_hbm,
    q_ref, kv_ref, o_ref, st_ref, s_ref, peak_ref, job_ref, q_sem, load_sem, store_sem, out_sem,
):
    requests, span = kv_ref.shape[0], kv_ref.shape[2]
    few = o_ref.shape[0]
    base = lax.axis_index("seq") * span

    def row_of(i):
        return 4 * (i % 4) + i // 4

    def q_load(i):
        rows = pl.ds(pl.multiple_of(row_of(i) * Q, Q), Q)
        return pltpu.make_async_copy(q_hbm.at[rows, :], q_ref.at[i], q_sem.at[i])

    def load(i):
        return pltpu.make_async_copy(kv_hbm.at[:, row_of(i)], kv_ref.at[i], load_sem.at[i])

    def store(i):
        return pltpu.make_async_copy(kv_ref.at[i], nc_hbm.at[:, row_of(i)], store_sem.at[i])

    def live(i):
        return jnp.clip(len_ref[row_of(i)] - base, 0, span)

    def begin(i, _):
        load(i).start()

        @pl.when(i < few)
        def _():
            q_load(i).start()

        return 0

    lax.fori_loop(0, requests, begin, 0)

    def listed(i, count):
        alive = live(i) > 0

        @pl.when(alive)
        def _():
            job_ref[count] = i

        @pl.when(jnp.logical_not(alive))
        def _():
            o_ref[i] = jnp.zeros(o_ref.shape[1:], o_ref.dtype)
            st_ref[i, 0:1] = jnp.full((1, st_ref.shape[2]), DEAD, jnp.float32)
            st_ref[i, 1:2] = jnp.zeros((1, st_ref.shape[2]), jnp.float32)

        return count + jnp.where(alive, 1, 0)

    job_ref[0] = 0
    jobs = lax.fori_loop(0, few, listed, 0)

    def arrive(i, _):
        load(i).wait()
        store(i).start()

        @pl.when(i < few)
        def _():
            q_load(i).wait()

        return 0

    def job(n):
        return job_ref[jnp.clip(n, 0, jnp.maximum(jobs - 1, 0))]

    @pl.when(jobs > 0)
    def _():
        first = job(0)
        lax.fori_loop(0, first + 1, arrive, 0)
        _, peak = attention_step(
            None, s_ref.at[0], None, kv_ref.at[first], stacked_heads(q_ref[first]), live(first), s_ref.at[0]
        )
        peak_ref[0:1] = peak

        def pair(n, _):
            for u in range(2):
                now, later = job(2 * n + u), job(2 * n + u + 1)
                lax.fori_loop(now + 1, later + 1, arrive, 0)
                peak = peak_ref[u : u + 1]
                acc, above = attention_step(
                    kv_ref.at[now], s_ref.at[u], peak,
                    kv_ref.at[later], stacked_heads(q_ref[later]), live(later), s_ref.at[1 - u],
                )
                publish(o_ref.at[now], st_ref.at[now], peak, acc)
                peak_ref[1 - u : 2 - u] = above
            lax.fori_loop(few + 2 * n, few + 2 * n + 2, arrive, 0)
            return 0

        lax.fori_loop(0, (jobs + 1) // 2, pair, 0)

    lax.fori_loop(jnp.where(jobs > 0, job(jobs) + 1, 0), few, arrive, 0)
    lax.fori_loop(few + (jobs + 1) // 2 * 2, requests, arrive, 0)
    outs = [
        pltpu.make_async_copy(o_ref, o_hbm, out_sem.at[0]),
        pltpu.make_async_copy(st_ref, st_hbm, out_sem.at[1]),
    ]
    for copy in outs:
        copy.start()

    def end(i, _):
        store(i).wait()
        return 0

    lax.fori_loop(0, requests, end, 0)
    for copy in outs:
        copy.wait()


def attend(lengths, queries, cache):
    requests, span = cache.shape[1], cache.shape[2]
    wide = queries.shape[1]
    width = wide // HEAD * Q
    few = requests // 2
    dma = pltpu.SemaphoreType.DMA
    far = pl.BlockSpec(memory_space=pl.ANY)
    o = jax.ShapeDtypeStruct((few, HEAD, width), jnp.bfloat16)
    st = jax.ShapeDtypeStruct((few, 8, width), jnp.float32)
    return pl.pallas_call(
        attend_kernel,
        out_shape=(o, st, jax.ShapeDtypeStruct(cache.shape, cache.dtype)),
        in_specs=[pl.BlockSpec(memory_space=pltpu.SMEM), far, far],
        out_specs=(far, far, far),
        scratch_shapes=[
            pltpu.VMEM((few, Q, wide), jnp.bfloat16),
            pltpu.VMEM((requests, 2, span, HEAD), jnp.bfloat16),
            pltpu.VMEM(o.shape, o.dtype),
            pltpu.VMEM(st.shape, st.dtype),
            pltpu.VMEM((2, span, width), jnp.float32),
            pltpu.VMEM((8, width), jnp.float32),
            pltpu.SMEM((few,), jnp.int32),
            dma((few,)),
            dma((requests,)),
            dma((requests,)),
            dma((2,)),
        ],
        compiler_params=pltpu.CompilerParams(vmem_limit_bytes=60 << 20),
        name="attend",
    )(lengths, queries, cache)


def commit_kernel(
    len_ref, acc_ref, chosen_ref, attn_ref, nc_in, out_ref, nc_ref, win_ref, load_sem, store_sem
):
    requests, span = nc_ref.shape[1], nc_ref.shape[2]
    base = lax.axis_index("seq") * span

    def place(r):
        off = len_ref[r] - base
        hit = (off + acc_ref[r] > 0) & (off < span)
        start = pl.multiple_of(jnp.clip(off // 16 * 16, 0, span - WINDOW), 16)
        return off, hit, start

    def load(r, start):
        return pltpu.make_async_copy(
            nc_ref.at[:, r, pl.ds(start, WINDOW), :], win_ref.at[r], load_sem.at[r]
        )

    def store(r, start):
        return pltpu.make_async_copy(
            win_ref.at[r], nc_ref.at[:, r, pl.ds(start, WINDOW), :], store_sem.at[r]
        )

    def begin(r, _):
        off, hit, start = place(r)

        @pl.when(hit)
        def _():
            load(r, start).start()

        return 0

    def change(r, _):
        off, hit, start = place(r)

        @pl.when(hit)
        def _():
            row = lax.broadcasted_iota(jnp.int32, (WINDOW, 2 * ACC), 0) + (start - off)
            node = lax.broadcasted_iota(jnp.int32, (WINDOW, 2 * ACC), 1)
            pick = jnp.where(row == node, 1.0, 0.0).astype(jnp.bfloat16)
            slot = lax.broadcasted_iota(jnp.int32, (WINDOW, HEAD), 0) + (start - off)
            fresh = (slot >= 0) & (slot < acc_ref[r])
            load(r, start).wait()
            for x in range(2):
                rows = jnp.dot(
                    pick,
                    chosen_ref[r, 2 * ACC * x : 2 * ACC * (x + 1)],
                    preferred_element_type=jnp.float32,
                )
                old = win_ref[r, x].astype(jnp.float32)
                win_ref[r, x] = jnp.where(fresh, rows, old).astype(jnp.bfloat16)
            store(r, start).start()

        return 0

    def end(r, _):
        off, hit, start = place(r)

        @pl.when(hit)
        def _():
            store(r, start).wait()

        return 0

    lax.fori_loop(0, requests, begin, 0)
    out_ref[...] = attn_ref[...]
    lax.fori_loop(0, requests, change, 0)
    lax.fori_loop(0, requests, end, 0)


def commit(lengths, accepted, chosen, attn, new_cache):
    requests = new_cache.shape[1]
    return pl.pallas_call(
        commit_kernel,
        out_shape=(
            jax.ShapeDtypeStruct(attn.shape, attn.dtype),
            jax.ShapeDtypeStruct(new_cache.shape, new_cache.dtype),
        ),
        in_specs=[pl.BlockSpec(memory_space=pltpu.SMEM)] * 2
        + [pl.BlockSpec(memory_space=pltpu.VMEM)] * 2
        + [pl.BlockSpec(memory_space=pl.ANY)],
        out_specs=(pl.BlockSpec(memory_space=pltpu.VMEM), pl.BlockSpec(memory_space=pl.ANY)),
        scratch_shapes=[
            pltpu.VMEM((requests, 2, WINDOW, HEAD), jnp.bfloat16),
            pltpu.SemaphoreType.DMA((requests,)),
            pltpu.SemaphoreType.DMA((requests,)),
        ],
        input_output_aliases={4: 1},
        name="commit",
    )(lengths, accepted, chosen, attn, new_cache)


def folded_parts(first, second):
    peak = jnp.maximum(first[0], second[0])
    a, b = jnp.exp2(first[0] - peak), jnp.exp2(second[0] - peak)
    return peak, first[1] * a + second[1] * b, a, b


def join_kernel(
    len_ref, o_hbm, st_hbm, q_hbm, kv_hbm, dkv_ref, par_ref, path_ref, w_hbm, out_ref, chosen_ref,
    q_ref, qs_ref, kv_ref, s_ref, peak_ref, o_ref, st_ref, w_ref, pair_o, pair_st, merge_o, merge_st, acc_ref, run_ref, att, rs_send, rs_recv,
    q_sem, qs_sem, kv_sem, in_sem, pair_ss, pair_rs, merge_ss, merge_rs, own_ss, relay_ss, pass_ss, att_rs, out_ss, out_rs,
):
    s, t = lax.axis_index("seq"), lax.axis_index("tp")
    k, c = s // 2, s % 2
    y, z = k // 4, k % 4
    chips, tps = pair_o.shape[0], rs_send.shape[0]
    partner = 2 * k + 1 - c
    width = o_ref.shape[2]
    heads = width // Q

    barrier = pltpu.get_barrier_semaphore()
    for d in range(1, chips):
        pl.semaphore_signal(barrier, inc=1, device_id={"seq": 2 * ((k + d) % chips) + c}, device_id_type=MESH)
    pl.semaphore_signal(barrier, inc=1, device_id={"seq": partner}, device_id_type=MESH)
    for d in range(1, tps):
        pl.semaphore_signal(barrier, inc=1, device_id={"tp": (t + d) % tps}, device_id_type=MESH)
    few, span = o_hbm.shape[0], kv_ref.shape[2]
    jobs = jnp.where(k < 4, kv_ref.shape[0], kv_ref.shape[0] // 2)

    def place(i):
        return 3 - i // 4, i % 4

    def row_of(i):
        tenant, turn = place(i)
        return 4 * turn + tenant

    def live(i):
        return jnp.clip(len_ref[row_of(i)] - s * span, 0, span)

    def qs_load(i):
        rows = pl.ds(pl.multiple_of(row_of(i) * Q, Q), Q)
        return pltpu.make_async_copy(q_hbm.at[rows, :], qs_ref.at[i], qs_sem.at[i])

    def kv_load(i):
        return pltpu.make_async_copy(kv_hbm.at[:, row_of(i)], kv_ref.at[i], kv_sem.at[i])

    q_copy = pltpu.make_async_copy(q_hbm.at[pl.ds(pl.multiple_of(s * Q, Q), Q), :], q_ref, q_sem)
    q_copy.start()

    def start_load(i, _):
        qs_load(i).start()
        kv_load(i).start()
        return 0

    lax.fori_loop(0, jobs, start_load, 0)
    w_copy = pltpu.make_async_copy(w_hbm, w_ref, in_sem.at[0])
    o_copy = pltpu.make_async_copy(o_hbm, o_ref.at[pl.ds(0, few)], in_sem.at[1])
    st_copy = pltpu.make_async_copy(st_hbm, st_ref.at[pl.ds(0, few)], in_sem.at[2])
    for copy in (o_copy, st_copy, w_copy):
        copy.start()

    def send(src, dst, ss, rs, **where):
        return pltpu.make_async_remote_copy(
            src_ref=src, dst_ref=dst, send_sem=ss, recv_sem=rs, device_id=where, device_id_type=MESH
        )

    def pair_copies(j):
        r = 4 * (2 * (j % 2) + 1 - c) + j // 2
        return (
            send(o_ref.at[r], pair_o.at[j], pair_ss.at[j, 0], pair_rs.at[j, 0], seq=partner),
            send(st_ref.at[r], pair_st.at[j], pair_ss.at[j, 1], pair_rs.at[j, 1], seq=partner),
        )

    def merge_copies(j):
        return (
            send(pair_o.at[j], merge_o.at[k], merge_ss.at[j, 0], merge_rs.at[k, 0], seq=2 * j + c),
            send(pair_st.at[j], merge_st.at[k], merge_ss.at[j, 1], merge_rs.at[k, 1], seq=2 * j + c),
        )

    def merge_arrival(i):
        return (
            send(pair_o.at[i], merge_o.at[i], merge_ss.at[i, 0], merge_rs.at[i, 0], seq=partner),
            send(pair_st.at[i], merge_st.at[i], merge_ss.at[i, 1], merge_rs.at[i, 1], seq=partner),
        )

    def pass_on(slot, ss, where):
        return send(att.at[slot], att.at[slot], ss, att_rs.at[slot], seq=where)

    def ring(d):
        return 2 * (y * 4 + (z + d) % 4) + c

    def out_copy(g):
        return send(rs_send.at[g], rs_recv.at[t], out_ss.at[g], out_rs.at[t], tp=g)

    def out_arrival(i):
        return send(rs_send.at[i], rs_recv.at[i], out_ss.at[i], out_rs.at[i], seq=partner)

    def reach_of(j, parity):
        return (1 + 3 * (j % 2)) * (1 + parity)

    node = lax.broadcasted_iota(jnp.int32, (Q, Q), 0)
    other = lax.broadcasted_iota(jnp.int32, (Q, Q), 1)
    parent = jnp.broadcast_to(par_ref[pl.ds(s, 1), :], (Q, Q))
    reach = jnp.where((node == other) | (node == parent), 1.0, 0.0)
    for _ in range((Q - 1).bit_length()):
        bits = reach.astype(jnp.bfloat16)
        reach = jnp.minimum(jnp.dot(bits, bits, preferred_element_type=jnp.float32), 1.0)
    lane = lax.broadcasted_iota(jnp.int32, (Q, width), 1) % Q
    spread = jnp.where(lane == lax.broadcasted_iota(jnp.int32, (Q, width), 0), 1.0, 0.0).astype(jnp.bfloat16)
    alive = jnp.dot(reach.astype(jnp.bfloat16), spread, preferred_element_type=jnp.float32) > 0.5
    q_copy.wait()
    scores = lax.dot_general(
        dkv_ref[0], stacked_heads(q_ref[...]), (((1,), (1,)), ((), ())), preferred_element_type=jnp.float32
    )
    scores = jnp.where(alive, scores, DEAD)
    peak = jnp.max(scores, axis=0, keepdims=True) * SCALE
    weights = jnp.where(alive, jnp.exp2(scores * SCALE - peak), 0.0)
    run_ref[0:1] = peak
    run_ref[1:2] = jnp.sum(weights, axis=0, keepdims=True)
    acc_ref[...] = jnp.dot(dkv_ref[1].T, weights.astype(jnp.bfloat16), preferred_element_type=jnp.float32)

    def combine(tenant, turn):
        j = 2 * turn + tenant // 2
        r = 4 * tenant + turn
        for copy in pair_copies(j):
            copy.wait_recv()
        peak, total, a, b = folded_parts((st_ref[r, 0:1], st_ref[r, 1:2]), (pair_st[j, 0:1], pair_st[j, 1:2]))
        mixed = o_ref[r].astype(jnp.float32) * a + pair_o[j].astype(jnp.float32) * b
        pair_o[j] = mixed.astype(jnp.bfloat16)
        pair_st[j, 0:1] = peak
        pair_st[j, 1:2] = total

        @pl.when(j != k)
        def _():
            for copy in merge_copies(j):
                copy.start()

    def combine_all(tenant):
        def each(turn, _):
            combine(tenant, (turn + k // 2) % 4)
            return 0

        @pl.when((tenant % 2 == c) & (k < 2**tenant))
        def _():
            lax.fori_loop(0, 4, each, 0)

    def start_pair(tenant, turn):
        @pl.when((tenant % 2 != c) & (k < reach_of(tenant // 2, tenant % 2)))
        def _():
            for copy in pair_copies(2 * turn + tenant // 2):
                copy.start()

    qs_load(0).wait()
    kv_load(0).wait()
    _, above = attention_step(
        None, s_ref.at[0], None, kv_ref.at[0], stacked_heads(qs_ref[0]), live(0), s_ref.at[0]
    )
    peak_ref[0:1] = above
    o_copy.wait()
    st_copy.wait()
    pl.semaphore_wait(barrier, chips + tps - 1)
    for tenant in range(2):
        for turn in range(4):
            start_pair(tenant, turn)

    def attend_pair(n, _):
        for u in range(2):
            now = 2 * n + u
            later = jnp.where(now + 1 < jobs, now + 1, 0)

            @pl.when(now + 1 < jobs)
            def _():
                qs_load(later).wait()
                kv_load(later).wait()

            peak = peak_ref[u : u + 1]
            acc, above = attention_step(
                kv_ref.at[now], s_ref.at[u], peak,
                kv_ref.at[later], stacked_heads(qs_ref[later]), live(later), s_ref.at[1 - u],
            )
            tenant, turn = place(now)
            publish(o_ref.at[4 * tenant + turn], st_ref.at[4 * tenant + turn], peak, acc)
            peak_ref[1 - u : 2 - u] = above
            start_pair(tenant, turn)

        @pl.when(n == 1)
        def _():
            combine_all(0)
            combine_all(1)

        @pl.when(n == 2)
        def _():
            combine_all(3)

        return 0

    lax.fori_loop(0, jobs // 2, attend_pair, 0)

    @pl.when(k < 4)
    def _():
        combine_all(2)

    @pl.when(k >= 4)
    def _():
        combine_all(3)

    def absorb(o, st):
        peak, total, a, b = folded_parts((run_ref[0:1], run_ref[1:2]), (st[0:1], st[1:2]))
        acc_ref[...] = acc_ref[...] * a + o[...].astype(jnp.float32) * b
        run_ref[0:1] = peak
        run_ref[1:2] = total

    def merge(i, _):
        j = (k + i) % chips

        @pl.when(j < reach_of(k, c))
        def _():
            @pl.when(j == k)
            def _():
                absorb(pair_o.at[j], pair_st.at[j])

            @pl.when(j != k)
            def _():
                for copy in merge_arrival(j):
                    copy.wait_recv()
                absorb(merge_o.at[j], merge_st.at[j])

        return 0

    lax.fori_loop(0, chips, merge, 0)

    att[s, :width] = (acc_ref[...] / run_ref[1:2]).T.astype(jnp.bfloat16)
    lanes = lax.broadcasted_iota(jnp.int32, path_ref.shape, 1)
    nodes = jnp.sum(jnp.where(lanes == s, path_ref[...], 0), axis=1, keepdims=True)
    pick = jnp.where(lax.broadcasted_iota(jnp.int32, (ACC, Q), 1) == nodes, 1.0, 0.0)
    pick = jnp.concatenate([pick, jnp.zeros((ACC, Q), jnp.float32)], axis=0).astype(jnp.bfloat16)
    for x in range(2):
        rows = jnp.dot(pick, dkv_ref[x], preferred_element_type=jnp.float32)
        att[s, width + 2 * ACC * x : width + 2 * ACC * (x + 1)] = rows.astype(jnp.bfloat16)

    twin = (k + 4) % chips
    own = [pass_on(s, own_ss.at[0], 2 * twin + c)]
    own += [pass_on(s, own_ss.at[d], ring(d)) for d in (1, 3, 2)]
    own += [pass_on(s, own_ss.at[4], partner)]
    for copy in own:
        copy.start()

    def group(i):
        return (y + i // 2) % 2 * 4 + (z // 2 * 2 + 2 * i + i // 4) % 4

    def forward(g):
        return pass_on(2 * g + c, pass_ss.at[g], partner)

    def relays():
        return [pass_on(2 * twin + c, relay_ss.at[d], ring(d)) for d in (1, 3, 2)]

    def arrival(slot):
        return pass_on(slot, own_ss.at[0], partner)

    def project(g):
        arrival(2 * g + 1 - c).wait_recv()
        rows = jnp.concatenate(
            [
                jnp.concatenate([att[2 * g, h * Q : (h + 1) * Q], att[2 * g + 1, h * Q : (h + 1) * Q]], axis=0)
                for h in range(heads)
            ],
            axis=1,
        )
        rs_send[g] = jnp.dot(rows, w_ref[...], preferred_element_type=jnp.float32).astype(jnp.bfloat16)

        @pl.when(g != t)
        def _():
            out_copy(g).start()

    def spread_on(i, _):
        g = group(i)

        @pl.when(g != k)
        def _():
            arrival(2 * g + c).wait_recv()
            forward(g).start()

        @pl.when(g == twin)
        def _():
            for copy in relays():
                copy.start()

        @pl.when(i > 0)
        def _():
            project(group(i - 1))

        return 0

    w_copy.wait()
    lax.fori_loop(0, chips, spread_on, 0)
    project(group(chips - 1))

    total = rs_send[t].astype(jnp.float32)
    for d in range(1, tps):
        i = (t + d) % tps
        out_arrival(i).wait_recv()
        total = total + rs_recv[i].astype(jnp.float32)
    out_ref[...] = total.astype(out_ref.dtype)
    chosen_ref[...] = att[:, width:]

    def finish_pair(j, _):
        @pl.when(k < reach_of(j, 1 - c))
        def _():
            for copy in pair_copies(j):
                copy.wait_send()

        @pl.when((k < reach_of(j, c)) & (j != k))
        def _():
            for copy in merge_copies(j):
                copy.wait_send()

        @pl.when(j != k)
        def _():
            forward(j).wait_send()

        @pl.when(j != t)
        def _():
            out_copy(j).wait_send()

        return 0

    lax.fori_loop(0, chips, finish_pair, 0)
    for copy in own + relays():
        copy.wait_send()


def join(lengths, o, st, queries, cache, draft_kv, parents, path, out_weight, chips, tps):
    requests, span = cache.shape[1], cache.shape[2]
    few, _, width = o.shape
    wide, columns = queries.shape[1], out_weight.shape[1]
    dma = pltpu.SemaphoreType.DMA
    whole, far = pl.BlockSpec(memory_space=pltpu.VMEM), pl.BlockSpec(memory_space=pl.ANY)
    return pl.pallas_call(
        join_kernel,
        out_shape=(
            jax.ShapeDtypeStruct((queries.shape[0] // tps, columns), jnp.bfloat16),
            jax.ShapeDtypeStruct((requests, 4 * ACC, HEAD), jnp.bfloat16),
        ),
        in_specs=[pl.BlockSpec(memory_space=pltpu.SMEM), far, far, far, far, whole, whole, whole, far],
        out_specs=(whole, whole),
        scratch_shapes=[
            pltpu.VMEM((Q, wide), jnp.bfloat16),
            pltpu.VMEM((requests // 2, Q, wide), jnp.bfloat16),
            pltpu.VMEM((requests // 2, 2, span, HEAD), jnp.bfloat16),
            pltpu.VMEM((2, span, width), jnp.float32),
            pltpu.VMEM((8, width), jnp.float32),
            pltpu.VMEM((requests, HEAD, width), o.dtype),
            pltpu.VMEM((requests, 8, width), st.dtype),
            pltpu.VMEM(out_weight.shape, out_weight.dtype),
            pltpu.VMEM((chips, HEAD, width), jnp.bfloat16),
            pltpu.VMEM((chips, 8, width), jnp.float32),
            pltpu.VMEM((chips, HEAD, width), jnp.bfloat16),
            pltpu.VMEM((chips, 8, width), jnp.float32),
            pltpu.VMEM((HEAD, width), jnp.float32),
            pltpu.VMEM((8, width), jnp.float32),
            pltpu.VMEM((requests, width + 4 * ACC, HEAD), jnp.bfloat16),
            pltpu.VMEM((tps, 2 * Q, columns), jnp.bfloat16),
            pltpu.VMEM((tps, 2 * Q, columns), jnp.bfloat16),
            dma,
            dma((requests // 2,)),
            dma((requests // 2,)),
            dma((3,)),
            dma((chips, 2)),
            dma((chips, 2)),
            dma((chips, 2)),
            dma((chips, 2)),
            dma((5,)),
            dma((4,)),
            dma((chips,)),
            dma((requests,)),
            dma((tps,)),
            dma((tps,)),
        ],
        compiler_params=pltpu.CompilerParams(
            collective_id=0, has_side_effects=True, vmem_limit_bytes=60 << 20
        ),
        name="join",
    )(lengths, o, st, queries, cache, draft_kv, parents, path, out_weight)


def solution(mesh):
    chips, tps = mesh.shape["seq"] // 2, mesh.shape["tp"]

    def local(queries, cache, draft_kv, out_weight, lengths, parents, path, accepted):
        o, st, new_cache = attend(lengths, queries, cache)
        attn, chosen = join(lengths, o, st, queries, cache, draft_kv, parents, path.T, out_weight, chips, tps)
        return commit(lengths, accepted, chosen, attn, new_cache)

    return jax.shard_map(
        local,
        mesh=mesh,
        in_specs=(
            P(None, "tp"),
            P(None, None, "seq", "tp"),
            P(None, "seq", "tp"),
            P("tp", "seq"),
            P(),
            P(),
            P(),
            P(),
        ),
        out_specs=(P("tp", "seq"), P(None, None, "seq", "tp")),
        check_vma=False,
    )
```

```python
import functools

import jax
import jax.numpy as jnp
from jax import lax
from jax.experimental import pallas as pl
from jax.experimental.pallas import tpu as pltpu
from jax.sharding import PartitionSpec as P

HEAD = 128
Q = 64
ACC = 8
MESH = pl.DeviceIdType.MESH
SCALE = HEAD**-0.5 * 1.4426950408889634
DEAD = -1e30
CHUNK = 256
WINDOW = 32


def stacked_heads(rows):
    heads = rows.shape[1] // HEAD
    return jnp.concatenate([rows[:, h * HEAD : (h + 1) * HEAD] for h in range(heads)], axis=0)


def score_chunk(kv, q, c, live):
    s = lax.dot_general(
        kv[0, c * CHUNK : (c + 1) * CHUNK, :], q, (((1,), (1,)), ((), ())), preferred_element_type=jnp.float32
    )
    row = lax.broadcasted_iota(jnp.int32, s.shape, 0) + c * CHUNK
    return jnp.where(row < live, s, DEAD)


def attention_step(now, s_now, peak_now, later, q_later, live, s_later):
    acc = peak = None
    for c in range(s_now.shape[0] // CHUNK):
        rows = slice(c * CHUNK, (c + 1) * CHUNK)
        if later is not None:
            s = score_chunk(later, q_later, c, live)
            s_later[rows, :] = s
            top = jnp.max(s.reshape(CHUNK // 8, 8, s.shape[1]), axis=0)
            peak = top if peak is None else jnp.maximum(peak, top)
        if now is not None:
            p = jnp.exp2(s_now[rows, :] * SCALE - peak_now).astype(jnp.bfloat16)
            values = now[1, rows, :].T
            values = jnp.concatenate([values, jnp.ones((16, CHUNK), values.dtype)], axis=0)
            term = jnp.dot(values, p, preferred_element_type=jnp.float32)
            acc = term if acc is None else acc + term
    if peak is not None:
        peak = jnp.max(peak, axis=0, keepdims=True) * SCALE
    return acc, peak


def publish(o, st, peak, acc):
    o[...] = acc[:HEAD].astype(o.dtype)
    st[0:1] = peak
    st[1:2] = acc[HEAD : HEAD + 1]


def attend_kernel(
    len_ref, q_hbm, kv_hbm, o_hbm, st_hbm, nc_hbm,
    q_ref, kv_ref, o_ref, st_ref, s_ref, peak_ref, job_ref, q_sem, load_sem, store_sem, out_sem,
):
    requests, span = kv_ref.shape[0], kv_ref.shape[2]
    few = o_ref.shape[0]
    base = lax.axis_index("seq") * span

    def row_of(i):
        return 4 * (i % 4) + i // 4

    def q_load(i):
        rows = pl.ds(pl.multiple_of(row_of(i) * Q, Q), Q)
        return pltpu.make_async_copy(q_hbm.at[rows, :], q_ref.at[i], q_sem.at[i])

    def load(i):
        return pltpu.make_async_copy(kv_hbm.at[:, row_of(i)], kv_ref.at[i], load_sem.at[i])

    def store(i):
        return pltpu.make_async_copy(kv_ref.at[i], nc_hbm.at[:, row_of(i)], store_sem.at[i])

    def live(i):
        return jnp.clip(len_ref[row_of(i)] - base, 0, span)

    def begin(i, _):
        load(i).start()

        @pl.when(i < few)
        def _():
            q_load(i).start()

        return 0

    lax.fori_loop(0, requests, begin, 0)

    def listed(i, count):
        alive = live(i) > 0

        @pl.when(alive)
        def _():
            job_ref[count] = i

        @pl.when(jnp.logical_not(alive))
        def _():
            o_ref[i] = jnp.zeros(o_ref.shape[1:], o_ref.dtype)
            st_ref[i, 0:1] = jnp.full((1, st_ref.shape[2]), DEAD, jnp.float32)
            st_ref[i, 1:2] = jnp.zeros((1, st_ref.shape[2]), jnp.float32)

        return count + jnp.where(alive, 1, 0)

    job_ref[0] = 0
    jobs = lax.fori_loop(0, few, listed, 0)

    def arrive(i, _):
        load(i).wait()
        store(i).start()

        @pl.when(i < few)
        def _():
            q_load(i).wait()

        return 0

    def job(n):
        return job_ref[jnp.clip(n, 0, jnp.maximum(jobs - 1, 0))]

    @pl.when(jobs > 0)
    def _():
        first = job(0)
        lax.fori_loop(0, first + 1, arrive, 0)
        _, peak = attention_step(
            None, s_ref.at[0], None, kv_ref.at[first], stacked_heads(q_ref[first]), live(first), s_ref.at[0]
        )
        peak_ref[0:1] = peak

        def pair(n, _):
            for u in range(2):
                now, later = job(2 * n + u), job(2 * n + u + 1)
                lax.fori_loop(now + 1, later + 1, arrive, 0)
                peak = peak_ref[u : u + 1]
                acc, above = attention_step(
                    kv_ref.at[now], s_ref.at[u], peak,
                    kv_ref.at[later], stacked_heads(q_ref[later]), live(later), s_ref.at[1 - u],
                )
                publish(o_ref.at[now], st_ref.at[now], peak, acc)
                peak_ref[1 - u : 2 - u] = above
            lax.fori_loop(few + 2 * n, few + 2 * n + 2, arrive, 0)
            return 0

        lax.fori_loop(0, (jobs + 1) // 2, pair, 0)

    lax.fori_loop(jnp.where(jobs > 0, job(jobs) + 1, 0), few, arrive, 0)
    lax.fori_loop(few + (jobs + 1) // 2 * 2, requests, arrive, 0)
    outs = [
        pltpu.make_async_copy(o_ref, o_hbm, out_sem.at[0]),
        pltpu.make_async_copy(st_ref, st_hbm, out_sem.at[1]),
    ]
    for copy in outs:
        copy.start()

    def end(i, _):
        store(i).wait()
        return 0

    lax.fori_loop(0, requests, end, 0)
    for copy in outs:
        copy.wait()


def attend(lengths, queries, cache):
    requests, span = cache.shape[1], cache.shape[2]
    wide = queries.shape[1]
    width = wide // HEAD * Q
    few = requests // 2
    dma = pltpu.SemaphoreType.DMA
    far = pl.BlockSpec(memory_space=pl.ANY)
    o = jax.ShapeDtypeStruct((few, HEAD, width), jnp.bfloat16)
    st = jax.ShapeDtypeStruct((few, 8, width), jnp.float32)
    return pl.pallas_call(
        attend_kernel,
        out_shape=(o, st, jax.ShapeDtypeStruct(cache.shape, cache.dtype)),
        in_specs=[pl.BlockSpec(memory_space=pltpu.SMEM), far, far],
        out_specs=(far, far, far),
        scratch_shapes=[
            pltpu.VMEM((few, Q, wide), jnp.bfloat16),
            pltpu.VMEM((requests, 2, span, HEAD), jnp.bfloat16),
            pltpu.VMEM(o.shape, o.dtype),
            pltpu.VMEM(st.shape, st.dtype),
            pltpu.VMEM((2, span, width), jnp.float32),
            pltpu.VMEM((8, width), jnp.float32),
            pltpu.SMEM((few,), jnp.int32),
            dma((few,)),
            dma((requests,)),
            dma((requests,)),
            dma((2,)),
        ],
        compiler_params=pltpu.CompilerParams(vmem_limit_bytes=60 << 20),
        name="attend",
    )(lengths, queries, cache)


def commit_kernel(
    len_ref, acc_ref, chosen_ref, attn_ref, nc_in, out_ref, nc_ref, win_ref, load_sem, store_sem
):
    requests, span = nc_ref.shape[1], nc_ref.shape[2]
    base = lax.axis_index("seq") * span

    def place(r):
        off = len_ref[r] - base
        hit = (off + acc_ref[r] > 0) & (off < span)
        start = pl.multiple_of(jnp.clip(off // 16 * 16, 0, span - WINDOW), 16)
        return off, hit, start

    def load(r, start):
        return pltpu.make_async_copy(
            nc_ref.at[:, r, pl.ds(start, WINDOW), :], win_ref.at[r], load_sem.at[r]
        )

    def store(r, start):
        return pltpu.make_async_copy(
            win_ref.at[r], nc_ref.at[:, r, pl.ds(start, WINDOW), :], store_sem.at[r]
        )

    def begin(r, _):
        off, hit, start = place(r)

        @pl.when(hit)
        def _():
            load(r, start).start()

        return 0

    def change(r, _):
        off, hit, start = place(r)

        @pl.when(hit)
        def _():
            row = lax.broadcasted_iota(jnp.int32, (WINDOW, 2 * ACC), 0) + (start - off)
            node = lax.broadcasted_iota(jnp.int32, (WINDOW, 2 * ACC), 1)
            pick = jnp.where(row == node, 1.0, 0.0).astype(jnp.bfloat16)
            slot = lax.broadcasted_iota(jnp.int32, (WINDOW, HEAD), 0) + (start - off)
            fresh = (slot >= 0) & (slot < acc_ref[r])
            load(r, start).wait()
            for x in range(2):
                rows = jnp.dot(
                    pick,
                    chosen_ref[r, 2 * ACC * x : 2 * ACC * (x + 1)],
                    preferred_element_type=jnp.float32,
                )
                old = win_ref[r, x].astype(jnp.float32)
                win_ref[r, x] = jnp.where(fresh, rows, old).astype(jnp.bfloat16)
            store(r, start).start()

        return 0

    def end(r, _):
        off, hit, start = place(r)

        @pl.when(hit)
        def _():
            store(r, start).wait()

        return 0

    lax.fori_loop(0, requests, begin, 0)
    out_ref[...] = attn_ref[...]
    lax.fori_loop(0, requests, change, 0)
    lax.fori_loop(0, requests, end, 0)


def commit(lengths, accepted, chosen, attn, new_cache):
    requests = new_cache.shape[1]
    return pl.pallas_call(
        commit_kernel,
        out_shape=(
            jax.ShapeDtypeStruct(attn.shape, attn.dtype),
            jax.ShapeDtypeStruct(new_cache.shape, new_cache.dtype),
        ),
        in_specs=[pl.BlockSpec(memory_space=pltpu.SMEM)] * 2
        + [pl.BlockSpec(memory_space=pltpu.VMEM)] * 2
        + [pl.BlockSpec(memory_space=pl.ANY)],
        out_specs=(pl.BlockSpec(memory_space=pltpu.VMEM), pl.BlockSpec(memory_space=pl.ANY)),
        scratch_shapes=[
            pltpu.VMEM((requests, 2, WINDOW, HEAD), jnp.bfloat16),
            pltpu.SemaphoreType.DMA((requests,)),
            pltpu.SemaphoreType.DMA((requests,)),
        ],
        input_output_aliases={4: 1},
        name="commit",
    )(lengths, accepted, chosen, attn, new_cache)


def folded_parts(first, second):
    peak = jnp.maximum(first[0], second[0])
    a, b = jnp.exp2(first[0] - peak), jnp.exp2(second[0] - peak)
    return peak, first[1] * a + second[1] * b, a, b


def join_kernel(
    len_ref, o_hbm, st_hbm, q_hbm, kv_hbm, dkv_ref, par_ref, path_ref, w_hbm, out_ref, chosen_ref,
    q_ref, qs_ref, kv_ref, s_ref, peak_ref, o_ref, st_ref, w_ref, pair_o, pair_st, merge_o, merge_st, acc_ref, run_ref, att, rs_send, rs_recv, half_ref,
    q_sem, qs_sem, kv_sem, in_sem, pair_ss, pair_rs, merge_ss, merge_rs, own_ss, pass_ss, att_rs, out_ss, out_rs, half_sem,
):
    s, t = lax.axis_index("seq"), lax.axis_index("tp")
    k, c = s // 2, s % 2
    y, z = k // 4, k % 4
    lx, across = t % 4, (t + 4) % 8
    chips, tps = pair_o.shape[0], rs_send.shape[0]
    partner = 2 * k + 1 - c
    width = o_ref.shape[2]
    heads = width // Q

    barrier = pltpu.get_barrier_semaphore()
    for d in range(1, chips):
        pl.semaphore_signal(barrier, inc=1, device_id={"seq": 2 * ((k + d) % chips) + c}, device_id_type=MESH)
    pl.semaphore_signal(barrier, inc=1, device_id={"seq": partner}, device_id_type=MESH)
    for d in range(1, tps):
        pl.semaphore_signal(barrier, inc=1, device_id={"tp": (t + d) % tps}, device_id_type=MESH)
    few, span = o_hbm.shape[0], kv_ref.shape[2]
    jobs = jnp.where(k < 4, kv_ref.shape[0], kv_ref.shape[0] // 2)

    def place(i):
        return 3 - i // 4, i % 4

    def row_of(i):
        tenant, turn = place(i)
        return 4 * turn + tenant

    def live(i):
        return jnp.clip(len_ref[row_of(i)] - s * span, 0, span)

    def qs_load(i):
        rows = pl.ds(pl.multiple_of(row_of(i) * Q, Q), Q)
        return pltpu.make_async_copy(q_hbm.at[rows, :], qs_ref.at[i], qs_sem.at[i])

    def kv_load(i):
        return pltpu.make_async_copy(kv_hbm.at[:, row_of(i)], kv_ref.at[i], kv_sem.at[i])

    q_copy = pltpu.make_async_copy(q_hbm.at[pl.ds(pl.multiple_of(s * Q, Q), Q), :], q_ref, q_sem)
    q_copy.start()

    def start_load(i, _):
        qs_load(i).start()
        kv_load(i).start()
        return 0

    lax.fori_loop(0, jobs, start_load, 0)
    w_copy = pltpu.make_async_copy(w_hbm, w_ref, in_sem.at[0])
    o_copy = pltpu.make_async_copy(o_hbm, o_ref.at[pl.ds(0, few)], in_sem.at[1])
    st_copy = pltpu.make_async_copy(st_hbm, st_ref.at[pl.ds(0, few)], in_sem.at[2])
    for copy in (o_copy, st_copy, w_copy):
        copy.start()

    def send(src, dst, ss, rs, **where):
        return pltpu.make_async_remote_copy(
            src_ref=src, dst_ref=dst, send_sem=ss, recv_sem=rs, device_id=where, device_id_type=MESH
        )

    def pair_copies(j):
        r = 4 * (2 * (j % 2) + 1 - c) + j // 2
        return (
            send(o_ref.at[r], pair_o.at[j], pair_ss.at[j, 0], pair_rs.at[j, 0], seq=partner),
            send(st_ref.at[r, pl.ds(0, 2)], pair_st.at[j, pl.ds(0, 2)], pair_ss.at[j, 1], pair_rs.at[j, 1], seq=partner),
        )

    def merge_copies(j):
        return (
            send(pair_o.at[j], merge_o.at[k], merge_ss.at[j, 0], merge_rs.at[k, 0], seq=2 * j + c),
            send(pair_st.at[j, pl.ds(0, 2)], merge_st.at[k, pl.ds(0, 2)], merge_ss.at[j, 1], merge_rs.at[k, 1], seq=2 * j + c),
        )

    def merge_arrival(i):
        return (
            send(pair_o.at[i], merge_o.at[i], merge_ss.at[i, 0], merge_rs.at[i, 0], seq=partner),
            send(pair_st.at[i, pl.ds(0, 2)], merge_st.at[i, pl.ds(0, 2)], merge_ss.at[i, 1], merge_rs.at[i, 1], seq=partner),
        )

    def pass_on(slot, ss, where):
        return send(att.at[slot], att.at[slot], ss, att_rs.at[slot], seq=where)

    def ring(d):
        return 2 * (y * 4 + (z + d) % 4) + c

    def far_ring(d):
        return 2 * ((1 - y) * 4 + (z + d) % 4) + c

    def out_copy(g):
        slot = jnp.where(g % 2 == 1, t, g // 4 * 4 + lx)
        where = jnp.where(g % 2 == 1, g, t // 4 * 4 + g % 4)
        return send(rs_send.at[g], rs_recv.at[slot], out_ss.at[g], out_rs.at[slot], tp=where)

    def leaves(g):
        return jnp.where(g % 2 == 1, g != t, g % 4 != lx)

    def out_arrival(i):
        return send(rs_send.at[i], rs_recv.at[i], out_ss.at[i], out_rs.at[i], seq=partner)

    def reach_of(j, parity):
        return (1 + 3 * (j % 2)) * (1 + parity)

    node = lax.broadcasted_iota(jnp.int32, (Q, Q), 0)
    other = lax.broadcasted_iota(jnp.int32, (Q, Q), 1)
    parent = jnp.broadcast_to(par_ref[pl.ds(s, 1), :], (Q, Q))
    reach = jnp.where((node == other) | (node == parent), 1.0, 0.0)
    for _ in range((Q - 1).bit_length()):
        bits = reach.astype(jnp.bfloat16)
        reach = jnp.minimum(jnp.dot(bits, bits, preferred_element_type=jnp.float32), 1.0)
    lane = lax.broadcasted_iota(jnp.int32, (Q, width), 1) % Q
    spread = jnp.where(lane == lax.broadcasted_iota(jnp.int32, (Q, width), 0), 1.0, 0.0).astype(jnp.bfloat16)
    alive = jnp.dot(reach.astype(jnp.bfloat16), spread, preferred_element_type=jnp.float32) > 0.5
    q_copy.wait()
    scores = lax.dot_general(
        dkv_ref[0], stacked_heads(q_ref[...]), (((1,), (1,)), ((), ())), preferred_element_type=jnp.float32
    )
    scores = jnp.where(alive, scores, DEAD)
    peak = jnp.max(scores, axis=0, keepdims=True) * SCALE
    weights = jnp.where(alive, jnp.exp2(scores * SCALE - peak), 0.0)
    run_ref[0:1] = peak
    run_ref[1:2] = jnp.sum(weights, axis=0, keepdims=True)
    acc_ref[...] = jnp.dot(dkv_ref[1].T, weights.astype(jnp.bfloat16), preferred_element_type=jnp.float32)

    def combine(tenant, turn):
        j = 2 * turn + tenant // 2
        r = 4 * tenant + turn
        for copy in pair_copies(j):
            copy.wait_recv()
        peak, total, a, b = folded_parts((st_ref[r, 0:1], st_ref[r, 1:2]), (pair_st[j, 0:1], pair_st[j, 1:2]))
        mixed = o_ref[r].astype(jnp.float32) * a + pair_o[j].astype(jnp.float32) * b
        pair_o[j] = mixed.astype(jnp.bfloat16)
        pair_st[j, 0:1] = peak
        pair_st[j, 1:2] = total

        @pl.when(j != k)
        def _():
            for copy in merge_copies(j):
                copy.start()

    def combine_all(tenant):
        def each(turn, _):
            combine(tenant, (turn + k // 2) % 4)
            return 0

        @pl.when((tenant % 2 == c) & (k < 2**tenant))
        def _():
            lax.fori_loop(0, 4, each, 0)

    def start_pair(tenant, turn):
        @pl.when((tenant % 2 != c) & (k < reach_of(tenant // 2, tenant % 2)))
        def _():
            for copy in pair_copies(2 * turn + tenant // 2):
                copy.start()

    qs_load(0).wait()
    kv_load(0).wait()
    _, above = attention_step(
        None, s_ref.at[0], None, kv_ref.at[0], stacked_heads(qs_ref[0]), live(0), s_ref.at[0]
    )
    peak_ref[0:1] = above
    def attend_two(n):
        for u in range(2):
            now = 2 * n + u
            later = jnp.where(now + 1 < jobs, now + 1, 0)

            @pl.when(now + 1 < jobs)
            def _():
                qs_load(later).wait()
                kv_load(later).wait()

            peak = peak_ref[u : u + 1]
            acc, above = attention_step(
                kv_ref.at[now], s_ref.at[u], peak,
                kv_ref.at[later], stacked_heads(qs_ref[later]), live(later), s_ref.at[1 - u],
            )
            tenant, turn = place(now)
            publish(o_ref.at[4 * tenant + turn], st_ref.at[4 * tenant + turn], peak, acc)
            peak_ref[1 - u : 2 - u] = above

    attend_two(0)
    o_copy.wait()
    st_copy.wait()
    pl.semaphore_wait(barrier, chips + tps - 1)
    for tenant in range(2):
        for turn in range(4):
            start_pair(tenant, turn)

    def start_two(n):
        for u in range(2):
            start_pair(*place(2 * n + u))

    start_two(0)

    def attend_pair(n, _):
        attend_two(n)
        start_two(n)

        @pl.when(n == 1)
        def _():
            combine_all(0)
            combine_all(1)

        @pl.when(n == 2)
        def _():
            combine_all(3)

        return 0

    lax.fori_loop(1, jobs // 2, attend_pair, 0)

    @pl.when(k < 4)
    def _():
        combine_all(2)

    @pl.when(k >= 4)
    def _():
        combine_all(3)

    def absorb(o, st):
        peak, total, a, b = folded_parts((run_ref[0:1], run_ref[1:2]), (st[0:1], st[1:2]))
        acc_ref[...] = acc_ref[...] * a + o[...].astype(jnp.float32) * b
        run_ref[0:1] = peak
        run_ref[1:2] = total

    def merge(i, _):
        j = (k + i) % chips

        @pl.when(j < reach_of(k, c))
        def _():
            @pl.when(j == k)
            def _():
                absorb(pair_o.at[j], pair_st.at[j])

            @pl.when(j != k)
            def _():
                for copy in merge_arrival(j):
                    copy.wait_recv()
                absorb(merge_o.at[j], merge_st.at[j])

        return 0

    lax.fori_loop(0, chips, merge, 0)

    att[s, :width] = (acc_ref[...] / run_ref[1:2]).T.astype(jnp.bfloat16)
    lanes = lax.broadcasted_iota(jnp.int32, path_ref.shape, 1)
    nodes = jnp.sum(jnp.where(lanes == s, path_ref[...], 0), axis=1, keepdims=True)
    pick = jnp.where(lax.broadcasted_iota(jnp.int32, (ACC, Q), 1) == nodes, 1.0, 0.0)
    pick = jnp.concatenate([pick, jnp.zeros((ACC, Q), jnp.float32)], axis=0).astype(jnp.bfloat16)
    for x in range(2):
        rows = jnp.dot(pick, dkv_ref[x], preferred_element_type=jnp.float32)
        att[s, width + 2 * ACC * x : width + 2 * ACC * (x + 1)] = rows.astype(jnp.bfloat16)

    twin = (k + 4) % chips
    own = [pass_on(s, own_ss.at[0], 2 * twin + c)]
    own += [pass_on(s, own_ss.at[d], ring(d)) for d in (1, 3, 2)]
    own += [pass_on(s, own_ss.at[4], partner)]
    own += [pass_on(s, own_ss.at[4 + d], far_ring(d)) for d in (1, 3, 2)]
    for copy in own:
        copy.start()

    def group(i):
        return (y + i // 2) % 2 * 4 + (z // 2 * 2 + 2 * i + i // 4) % 4

    def forward(g):
        return pass_on(2 * g + c, pass_ss.at[g], partner)

    def arrival(slot):
        return pass_on(slot, own_ss.at[0], partner)

    def project(g):
        arrival(2 * g + 1 - c).wait_recv()
        rows = jnp.concatenate(
            [
                jnp.concatenate([att[2 * g, h * Q : (h + 1) * Q], att[2 * g + 1, h * Q : (h + 1) * Q]], axis=0)
                for h in range(heads)
            ],
            axis=1,
        )
        rs_send[g] = jnp.dot(rows, w_ref[...], preferred_element_type=jnp.float32).astype(jnp.bfloat16)

        @pl.when(leaves(g))
        def _():
            out_copy(g).start()

    def spread_on(i, _):
        g = group(i)

        @pl.when(g != k)
        def _():
            arrival(2 * g + c).wait_recv()
            forward(g).start()

        @pl.when(i > 0)
        def _():
            project(group(i - 1))

        return 0

    w_copy.wait()
    lax.fori_loop(0, chips, spread_on, 0)
    project(group(chips - 1))

    def gathered(g, slots):
        total = rs_send[g].astype(jnp.float32)
        for i in slots:
            out_arrival(i).wait_recv()
            total = total + rs_recv[i].astype(jnp.float32)
        return total

    def row_slots(g):
        return [g // 4 * 4 + (lx + d) % 4 for d in range(1, 4)]

    swap = send(half_ref.at[0], half_ref.at[1], half_sem.at[0], half_sem.at[1], tp=across)

    @pl.when(t % 2 == 0)
    def _():
        half_ref[0] = gathered(across, row_slots(across)).astype(jnp.bfloat16)
        swap.start()
        total = gathered(t, row_slots(t))
        swap.wait()
        out_ref[...] = (total + half_ref[1].astype(jnp.float32)).astype(out_ref.dtype)

    @pl.when(t % 2 == 1)
    def _():
        out_ref[...] = gathered(t, [(t + d) % tps for d in range(1, tps)]).astype(out_ref.dtype)

    chosen_ref[...] = att[:, width:]

    def finish_pair(j, _):
        @pl.when(k < reach_of(j, 1 - c))
        def _():
            for copy in pair_copies(j):
                copy.wait_send()

        @pl.when((k < reach_of(j, c)) & (j != k))
        def _():
            for copy in merge_copies(j):
                copy.wait_send()

        @pl.when(j != k)
        def _():
            forward(j).wait_send()

        @pl.when(leaves(j))
        def _():
            out_copy(j).wait_send()

        return 0

    lax.fori_loop(0, chips, finish_pair, 0)
    for copy in own:
        copy.wait_send()


def join(lengths, o, st, queries, cache, draft_kv, parents, path, out_weight, chips, tps):
    requests, span = cache.shape[1], cache.shape[2]
    few, _, width = o.shape
    wide, columns = queries.shape[1], out_weight.shape[1]
    dma = pltpu.SemaphoreType.DMA
    whole, far = pl.BlockSpec(memory_space=pltpu.VMEM), pl.BlockSpec(memory_space=pl.ANY)
    return pl.pallas_call(
        join_kernel,
        out_shape=(
            jax.ShapeDtypeStruct((queries.shape[0] // tps, columns), jnp.bfloat16),
            jax.ShapeDtypeStruct((requests, 4 * ACC, HEAD), jnp.bfloat16),
        ),
        in_specs=[pl.BlockSpec(memory_space=pltpu.SMEM), far, far, far, far, whole, whole, whole, far],
        out_specs=(whole, whole),
        scratch_shapes=[
            pltpu.VMEM((Q, wide), jnp.bfloat16),
            pltpu.VMEM((requests // 2, Q, wide), jnp.bfloat16),
            pltpu.VMEM((requests // 2, 2, span, HEAD), jnp.bfloat16),
            pltpu.VMEM((2, span, width), jnp.float32),
            pltpu.VMEM((8, width), jnp.float32),
            pltpu.VMEM((requests, HEAD, width), o.dtype),
            pltpu.VMEM((requests, 8, width), st.dtype),
            pltpu.VMEM(out_weight.shape, out_weight.dtype),
            pltpu.VMEM((chips, HEAD, width), jnp.bfloat16),
            pltpu.VMEM((chips, 8, width), jnp.float32),
            pltpu.VMEM((chips, HEAD, width), jnp.bfloat16),
            pltpu.VMEM((chips, 8, width), jnp.float32),
            pltpu.VMEM((HEAD, width), jnp.float32),
            pltpu.VMEM((8, width), jnp.float32),
            pltpu.VMEM((requests, width + 4 * ACC, HEAD), jnp.bfloat16),
            pltpu.VMEM((tps, 2 * Q, columns), jnp.bfloat16),
            pltpu.VMEM((tps, 2 * Q, columns), jnp.bfloat16),
            pltpu.VMEM((2, 2 * Q, columns), jnp.bfloat16),
            dma,
            dma((requests // 2,)),
            dma((requests // 2,)),
            dma((3,)),
            dma((chips, 2)),
            dma((chips, 2)),
            dma((chips, 2)),
            dma((chips, 2)),
            dma((8,)),
            dma((chips,)),
            dma((requests,)),
            dma((tps,)),
            dma((tps,)),
            dma((2,)),
        ],
        compiler_params=pltpu.CompilerParams(
            collective_id=0, has_side_effects=True, vmem_limit_bytes=60 << 20
        ),
        name="join",
    )(lengths, o, st, queries, cache, draft_kv, parents, path, out_weight)


def solution(mesh):
    chips, tps = mesh.shape["seq"] // 2, mesh.shape["tp"]

    def local(queries, cache, draft_kv, out_weight, lengths, parents, path, accepted):
        o, st, new_cache = attend(lengths, queries, cache)
        attn, chosen = join(lengths, o, st, queries, cache, draft_kv, parents, path.T, out_weight, chips, tps)
        return commit(lengths, accepted, chosen, attn, new_cache)

    return jax.shard_map(
        local,
        mesh=mesh,
        in_specs=(
            P(None, "tp"),
            P(None, None, "seq", "tp"),
            P(None, "seq", "tp"),
            P("tp", "seq"),
            P(),
            P(),
            P(),
            P(),
        ),
        out_specs=(P("tp", "seq"), P(None, None, "seq", "tp")),
        check_vma=False,
    )
```

```python
import functools

import jax
import jax.numpy as jnp
from jax import lax
from jax.experimental import pallas as pl
from jax.experimental.pallas import tpu as pltpu
from jax.sharding import PartitionSpec as P

HEAD = 128
Q = 64
ACC = 8
MESH = pl.DeviceIdType.MESH
SCALE = HEAD**-0.5 * 1.4426950408889634
DEAD = -1e30
CHUNK = 256
WINDOW = 32


def stacked_heads(rows):
    heads = rows.shape[1] // HEAD
    return jnp.concatenate([rows[:, h * HEAD : (h + 1) * HEAD] for h in range(heads)], axis=0)


def score_chunk(kv, q, c, live):
    s = lax.dot_general(
        kv[0, c * CHUNK : (c + 1) * CHUNK, :], q, (((1,), (1,)), ((), ())), preferred_element_type=jnp.float32
    )
    row = lax.broadcasted_iota(jnp.int32, s.shape, 0) + c * CHUNK
    return jnp.where(row < live, s, DEAD)


def attention_step(now, s_now, peak_now, later, q_later, live, s_later):
    acc = peak = None
    for c in range(s_now.shape[0] // CHUNK):
        rows = slice(c * CHUNK, (c + 1) * CHUNK)
        if later is not None:
            s = score_chunk(later, q_later, c, live)
            s_later[rows, :] = s
            top = jnp.max(s.reshape(CHUNK // 8, 8, s.shape[1]), axis=0)
            peak = top if peak is None else jnp.maximum(peak, top)
        if now is not None:
            p = jnp.exp2(s_now[rows, :] * SCALE - peak_now).astype(jnp.bfloat16)
            values = now[1, rows, :].T
            values = jnp.concatenate([values, jnp.ones((16, CHUNK), values.dtype)], axis=0)
            term = jnp.dot(values, p, preferred_element_type=jnp.float32)
            acc = term if acc is None else acc + term
    if peak is not None:
        peak = jnp.max(peak, axis=0, keepdims=True) * SCALE
    return acc, peak


def publish(o, st, peak, acc):
    o[...] = acc[:HEAD].astype(o.dtype)
    st[0:1] = peak
    st[1:2] = acc[HEAD : HEAD + 1]


def commit_kernel(
    len_ref, acc_ref, chosen_ref, attn_ref, kv_ref, out_ref, nc_ref, win_ref, store_sem, win_sem
):
    requests, span = kv_ref.shape[0], kv_ref.shape[2]
    base = lax.axis_index("seq") * span

    def held(r):
        return (3 - r % 4) * 4 + r // 4

    def place(r):
        off = len_ref[r] - base
        hit = (off + acc_ref[r] > 0) & (off < span)
        return off, hit, pl.multiple_of(jnp.clip(off // 16 * 16, 0, span - WINDOW), 16)

    def store(r):
        return pltpu.make_async_copy(kv_ref.at[held(r)], nc_ref.at[:, r], store_sem.at[r])

    def patch(r, start):
        return pltpu.make_async_copy(win_ref.at[r], nc_ref.at[:, r, pl.ds(start, WINDOW), :], win_sem.at[r])

    def begin(r, _):
        store(r).start()
        return 0

    def change(r, _):
        off, hit, start = place(r)

        @pl.when(hit)
        def _():
            row = lax.broadcasted_iota(jnp.int32, (WINDOW, 2 * ACC), 0) + (start - off)
            node = lax.broadcasted_iota(jnp.int32, (WINDOW, 2 * ACC), 1)
            pick = jnp.where(row == node, 1.0, 0.0).astype(jnp.bfloat16)
            slot = lax.broadcasted_iota(jnp.int32, (WINDOW, HEAD), 0) + (start - off)
            fresh = (slot >= 0) & (slot < acc_ref[r])
            for x in range(2):
                rows = jnp.dot(
                    pick,
                    chosen_ref[r, 2 * ACC * x : 2 * ACC * (x + 1)],
                    preferred_element_type=jnp.float32,
                )
                old = kv_ref[held(r), x, pl.ds(start, WINDOW), :].astype(jnp.float32)
                win_ref[r, x] = jnp.where(fresh, rows, old).astype(jnp.bfloat16)

        return 0

    def end(r, _):
        off, hit, start = place(r)
        store(r).wait()

        @pl.when(hit)
        def _():
            patch(r, start).start()

        return 0

    def close(r, _):
        off, hit, start = place(r)

        @pl.when(hit)
        def _():
            patch(r, start).wait()

        return 0

    lax.fori_loop(0, requests, begin, 0)
    out_ref[...] = attn_ref[...]
    lax.fori_loop(0, requests, change, 0)
    lax.fori_loop(0, requests, end, 0)
    lax.fori_loop(0, requests, close, 0)


def commit(lengths, accepted, chosen, attn, held, shape):
    requests = shape[1]
    near, far = pl.BlockSpec(memory_space=pltpu.VMEM), pl.BlockSpec(memory_space=pl.ANY)
    return pl.pallas_call(
        commit_kernel,
        out_shape=(
            jax.ShapeDtypeStruct(attn.shape, attn.dtype),
            jax.ShapeDtypeStruct(shape, held.dtype),
        ),
        in_specs=[pl.BlockSpec(memory_space=pltpu.SMEM)] * 2 + [near] * 3,
        out_specs=(near, far),
        scratch_shapes=[
            pltpu.VMEM((requests, 2, WINDOW, HEAD), jnp.bfloat16),
            pltpu.SemaphoreType.DMA((requests,)),
            pltpu.SemaphoreType.DMA((requests,)),
        ],
        compiler_params=pltpu.CompilerParams(vmem_limit_bytes=40 << 20),
        name="commit",
    )(lengths, accepted, chosen, attn, held)


def folded_parts(first, second):
    peak = jnp.maximum(first[0], second[0])
    a, b = jnp.exp2(first[0] - peak), jnp.exp2(second[0] - peak)
    return peak, first[1] * a + second[1] * b, a, b


def join_kernel(
    len_ref, q_hbm, kv_hbm, dkv_ref, par_ref, path_ref, w_hbm, out_ref, chosen_ref, kv_ref,
    q_ref, qs_ref, s_ref, peak_ref, o_ref, st_ref, w_ref, pair_o, pair_st, merge_o, merge_st, acc_ref, run_ref, att, rs_send, rs_recv, half_ref,
    q_sem, qs_sem, kv_sem, in_sem, pair_ss, pair_rs, merge_ss, merge_rs, own_ss, pass_ss, att_rs, out_ss, out_rs, half_sem,
):
    s, t = lax.axis_index("seq"), lax.axis_index("tp")
    k, c = s // 2, s % 2
    y, z = k // 4, k % 4
    lx, across = t % 4, (t + 4) % 8
    chips, tps = pair_o.shape[0], rs_send.shape[0]
    partner = 2 * k + 1 - c
    width = o_ref.shape[2]
    heads = width // Q

    barrier = pltpu.get_barrier_semaphore()
    for d in range(1, chips):
        pl.semaphore_signal(barrier, inc=1, device_id={"seq": 2 * ((k + d) % chips) + c}, device_id_type=MESH)
    pl.semaphore_signal(barrier, inc=1, device_id={"seq": partner}, device_id_type=MESH)
    for d in range(1, tps):
        pl.semaphore_signal(barrier, inc=1, device_id={"tp": (t + d) % tps}, device_id_type=MESH)
    span = kv_ref.shape[2]
    jobs = 4 * sum(jnp.where(k < 2**tenant, 1, 0) for tenant in range(4))

    def place(i):
        return 3 - i // 4, i % 4

    def row_of(i):
        tenant, turn = place(i)
        return 4 * turn + tenant

    def live(i):
        return jnp.clip(len_ref[row_of(i)] - s * span, 0, span)

    def qs_load(i):
        rows = pl.ds(pl.multiple_of(row_of(i) * Q, Q), Q)
        return pltpu.make_async_copy(q_hbm.at[rows, :], qs_ref.at[i], qs_sem.at[i])

    def kv_load(i):
        return pltpu.make_async_copy(kv_hbm.at[:, row_of(i)], kv_ref.at[i], kv_sem.at[i])

    q_copy = pltpu.make_async_copy(q_hbm.at[pl.ds(pl.multiple_of(s * Q, Q), Q), :], q_ref, q_sem)
    q_copy.start()

    def start_load(i, _):
        qs_load(i).start()
        kv_load(i).start()
        return 0

    lax.fori_loop(0, jobs, start_load, 0)

    def start_idle(i, _):
        kv_load(i).start()
        return 0

    lax.fori_loop(jobs, kv_ref.shape[0], start_idle, 0)
    w_copy = pltpu.make_async_copy(w_hbm, w_ref, in_sem)
    w_copy.start()

    def send(src, dst, ss, rs, **where):
        return pltpu.make_async_remote_copy(
            src_ref=src, dst_ref=dst, send_sem=ss, recv_sem=rs, device_id=where, device_id_type=MESH
        )

    def pair_copies(j):
        r = 4 * (2 * (j % 2) + 1 - c) + j // 2
        return (
            send(o_ref.at[r], pair_o.at[j], pair_ss.at[j, 0], pair_rs.at[j, 0], seq=partner),
            send(st_ref.at[r, pl.ds(0, 2)], pair_st.at[j, pl.ds(0, 2)], pair_ss.at[j, 1], pair_rs.at[j, 1], seq=partner),
        )

    def merge_copies(j):
        return (
            send(pair_o.at[j], merge_o.at[k], merge_ss.at[j, 0], merge_rs.at[k, 0], seq=2 * j + c),
            send(pair_st.at[j, pl.ds(0, 2)], merge_st.at[k, pl.ds(0, 2)], merge_ss.at[j, 1], merge_rs.at[k, 1], seq=2 * j + c),
        )

    def merge_arrival(i):
        return (
            send(pair_o.at[i], merge_o.at[i], merge_ss.at[i, 0], merge_rs.at[i, 0], seq=partner),
            send(pair_st.at[i, pl.ds(0, 2)], merge_st.at[i, pl.ds(0, 2)], merge_ss.at[i, 1], merge_rs.at[i, 1], seq=partner),
        )

    def pass_on(slot, ss, where):
        return send(att.at[slot], att.at[slot], ss, att_rs.at[slot], seq=where)

    def ring(d):
        return 2 * (y * 4 + (z + d) % 4) + c

    def far_ring(d):
        return 2 * ((1 - y) * 4 + (z + d) % 4) + c

    def out_copy(g):
        slot = jnp.where(g % 2 == 1, t, g // 4 * 4 + lx)
        where = jnp.where(g % 2 == 1, g, t // 4 * 4 + g % 4)
        return send(rs_send.at[g], rs_recv.at[slot], out_ss.at[g], out_rs.at[slot], tp=where)

    def leaves(g):
        return jnp.where(g % 2 == 1, g != t, g % 4 != lx)

    def out_arrival(i):
        return send(rs_send.at[i], rs_recv.at[i], out_ss.at[i], out_rs.at[i], seq=partner)

    def reach_of(j, parity):
        return (1 + 3 * (j % 2)) * (1 + parity)

    node = lax.broadcasted_iota(jnp.int32, (Q, Q), 0)
    other = lax.broadcasted_iota(jnp.int32, (Q, Q), 1)
    parent = jnp.broadcast_to(par_ref[pl.ds(s, 1), :], (Q, Q))
    reach = jnp.where((node == other) | (node == parent), 1.0, 0.0)
    for _ in range((Q - 1).bit_length()):
        bits = reach.astype(jnp.bfloat16)
        reach = jnp.minimum(jnp.dot(bits, bits, preferred_element_type=jnp.float32), 1.0)
    lane = lax.broadcasted_iota(jnp.int32, (Q, width), 1) % Q
    spread = jnp.where(lane == lax.broadcasted_iota(jnp.int32, (Q, width), 0), 1.0, 0.0).astype(jnp.bfloat16)
    alive = jnp.dot(reach.astype(jnp.bfloat16), spread, preferred_element_type=jnp.float32) > 0.5
    q_copy.wait()
    scores = lax.dot_general(
        dkv_ref[0], stacked_heads(q_ref[...]), (((1,), (1,)), ((), ())), preferred_element_type=jnp.float32
    )
    scores = jnp.where(alive, scores, DEAD)
    peak = jnp.max(scores, axis=0, keepdims=True) * SCALE
    weights = jnp.where(alive, jnp.exp2(scores * SCALE - peak), 0.0)
    run_ref[0:1] = peak
    run_ref[1:2] = jnp.sum(weights, axis=0, keepdims=True)
    acc_ref[...] = jnp.dot(dkv_ref[1].T, weights.astype(jnp.bfloat16), preferred_element_type=jnp.float32)

    def combine(tenant, turn):
        pl.when(tenant % 2 == c)(lambda: combine_now(tenant, turn))

    def combine_now(tenant, turn):
        j = 2 * turn + tenant // 2
        r = 4 * tenant + turn
        for copy in pair_copies(j):
            copy.wait_recv()
        peak, total, a, b = folded_parts((st_ref[r, 0:1], st_ref[r, 1:2]), (pair_st[j, 0:1], pair_st[j, 1:2]))
        mixed = o_ref[r].astype(jnp.float32) * a + pair_o[j].astype(jnp.float32) * b
        pair_o[j] = mixed.astype(jnp.bfloat16)
        pair_st[j, 0:1] = peak
        pair_st[j, 1:2] = total

        @pl.when(j != k)
        def _():
            for copy in merge_copies(j):
                copy.start()

    def start_pair(tenant, turn):
        @pl.when(tenant % 2 != c)
        def _():
            for copy in pair_copies(2 * turn + tenant // 2):
                copy.start()

    qs_load(0).wait()
    kv_load(0).wait()
    _, above = attention_step(
        None, s_ref.at[0], None, kv_ref.at[0], stacked_heads(qs_ref[0]), live(0), s_ref.at[0]
    )
    peak_ref[0:1] = above
    def attend_two(n):
        for u in range(2):
            now = 2 * n + u
            later = jnp.where(now + 1 < jobs, now + 1, 0)

            @pl.when(now + 1 < jobs)
            def _():
                qs_load(later).wait()
                kv_load(later).wait()

            peak = peak_ref[u : u + 1]
            acc, above = attention_step(
                kv_ref.at[now], s_ref.at[u], peak,
                kv_ref.at[later], stacked_heads(qs_ref[later]), live(later), s_ref.at[1 - u],
            )
            tenant, turn = place(now)
            publish(o_ref.at[4 * tenant + turn], st_ref.at[4 * tenant + turn], peak, acc)
            peak_ref[1 - u : 2 - u] = above

    attend_two(0)
    pl.semaphore_wait(barrier, chips + tps - 1)

    def start_two(n):
        for u in range(2):
            start_pair(*place(2 * n + u))

    start_two(0)

    def attend_pair(n, _):
        attend_two(n)
        start_two(n)

        for u in range(2):
            combine(*place(2 * n - 2 + u))
        return 0

    lax.fori_loop(1, jobs // 2, attend_pair, 0)
    for u in range(2):
        combine(*place(jobs - 2 + u))

    def absorb(o, st):
        peak, total, a, b = folded_parts((run_ref[0:1], run_ref[1:2]), (st[0:1], st[1:2]))
        acc_ref[...] = acc_ref[...] * a + o[...].astype(jnp.float32) * b
        run_ref[0:1] = peak
        run_ref[1:2] = total

    def merge(i, _):
        j = (k + i) % chips

        @pl.when(j < reach_of(k, c))
        def _():
            @pl.when(j == k)
            def _():
                absorb(pair_o.at[j], pair_st.at[j])

            @pl.when(j != k)
            def _():
                for copy in merge_arrival(j):
                    copy.wait_recv()
                absorb(merge_o.at[j], merge_st.at[j])

        return 0

    lax.fori_loop(0, chips, merge, 0)

    att[s, :width] = (acc_ref[...] / run_ref[1:2]).T.astype(jnp.bfloat16)
    lanes = lax.broadcasted_iota(jnp.int32, path_ref.shape, 1)
    nodes = jnp.sum(jnp.where(lanes == s, path_ref[...], 0), axis=1, keepdims=True)
    pick = jnp.where(lax.broadcasted_iota(jnp.int32, (ACC, Q), 1) == nodes, 1.0, 0.0)
    pick = jnp.concatenate([pick, jnp.zeros((ACC, Q), jnp.float32)], axis=0).astype(jnp.bfloat16)
    for x in range(2):
        rows = jnp.dot(pick, dkv_ref[x], preferred_element_type=jnp.float32)
        att[s, width + 2 * ACC * x : width + 2 * ACC * (x + 1)] = rows.astype(jnp.bfloat16)

    twin = (k + 4) % chips
    own = [pass_on(s, own_ss.at[0], 2 * twin + c)]
    own += [pass_on(s, own_ss.at[d], ring(d)) for d in (1, 3, 2)]
    own += [pass_on(s, own_ss.at[4], partner)]
    own += [pass_on(s, own_ss.at[4 + d], far_ring(d)) for d in (1, 3, 2)]
    for copy in own:
        copy.start()

    def group(i):
        return (y + i // 2) % 2 * 4 + (z // 2 * 2 + 2 * i + i // 4) % 4

    def forward(g):
        return pass_on(2 * g + c, pass_ss.at[g], partner)

    def arrival(slot):
        return pass_on(slot, own_ss.at[0], partner)

    def project(g):
        arrival(2 * g + 1 - c).wait_recv()
        rows = jnp.concatenate(
            [
                jnp.concatenate([att[2 * g, h * Q : (h + 1) * Q], att[2 * g + 1, h * Q : (h + 1) * Q]], axis=0)
                for h in range(heads)
            ],
            axis=1,
        )
        rs_send[g] = jnp.dot(rows, w_ref[...], preferred_element_type=jnp.float32).astype(jnp.bfloat16)

        @pl.when(leaves(g))
        def _():
            out_copy(g).start()

    def spread_on(i, _):
        g = group(i)

        @pl.when(g != k)
        def _():
            arrival(2 * g + c).wait_recv()
            forward(g).start()

        @pl.when(i > 0)
        def _():
            project(group(i - 1))

        return 0

    w_copy.wait()
    lax.fori_loop(0, chips, spread_on, 0)
    project(group(chips - 1))

    def gathered(g, slots):
        total = rs_send[g].astype(jnp.float32)
        for i in slots:
            out_arrival(i).wait_recv()
            total = total + rs_recv[i].astype(jnp.float32)
        return total

    def row_slots(g):
        return [g // 4 * 4 + (lx + d) % 4 for d in range(1, 4)]

    swap = send(half_ref.at[0], half_ref.at[1], half_sem.at[0], half_sem.at[1], tp=across)

    @pl.when(t % 2 == 0)
    def _():
        half_ref[0] = gathered(across, row_slots(across)).astype(jnp.bfloat16)
        swap.start()
        total = gathered(t, row_slots(t))
        swap.wait()
        out_ref[...] = (total + half_ref[1].astype(jnp.float32)).astype(out_ref.dtype)

    @pl.when(t % 2 == 1)
    def _():
        out_ref[...] = gathered(t, [(t + d) % tps for d in range(1, tps)]).astype(out_ref.dtype)

    chosen_ref[...] = att[:, width:]

    def finish_pair(j, _):
        @pl.when(k < reach_of(j, 1 - c))
        def _():
            for copy in pair_copies(j):
                copy.wait_send()

        @pl.when((k < reach_of(j, c)) & (j != k))
        def _():
            for copy in merge_copies(j):
                copy.wait_send()

        @pl.when(j != k)
        def _():
            forward(j).wait_send()

        @pl.when(leaves(j))
        def _():
            out_copy(j).wait_send()

        return 0

    lax.fori_loop(0, chips, finish_pair, 0)

    def finish_idle(i, _):
        kv_load(i).wait()
        return 0

    lax.fori_loop(jobs, kv_ref.shape[0], finish_idle, 0)
    for copy in own:
        copy.wait_send()


def join(lengths, queries, cache, draft_kv, parents, path, out_weight, chips, tps):
    requests, span = cache.shape[1], cache.shape[2]
    wide, columns = queries.shape[1], out_weight.shape[1]
    width = wide // HEAD * Q
    dma = pltpu.SemaphoreType.DMA
    whole, far = pl.BlockSpec(memory_space=pltpu.VMEM), pl.BlockSpec(memory_space=pl.ANY)
    return pl.pallas_call(
        join_kernel,
        out_shape=(
            jax.ShapeDtypeStruct((queries.shape[0] // tps, columns), jnp.bfloat16),
            jax.ShapeDtypeStruct((requests, 4 * ACC, HEAD), jnp.bfloat16),
            jax.ShapeDtypeStruct((requests, 2, span, HEAD), jnp.bfloat16),
        ),
        in_specs=[pl.BlockSpec(memory_space=pltpu.SMEM), far, far, whole, whole, whole, far],
        out_specs=(whole, whole, whole),
        scratch_shapes=[
            pltpu.VMEM((Q, wide), jnp.bfloat16),
            pltpu.VMEM((requests, Q, wide), jnp.bfloat16),
            pltpu.VMEM((2, span, width), jnp.float32),
            pltpu.VMEM((8, width), jnp.float32),
            pltpu.VMEM((requests, HEAD, width), jnp.bfloat16),
            pltpu.VMEM((requests, 8, width), jnp.float32),
            pltpu.VMEM(out_weight.shape, out_weight.dtype),
            pltpu.VMEM((chips, HEAD, width), jnp.bfloat16),
            pltpu.VMEM((chips, 8, width), jnp.float32),
            pltpu.VMEM((chips, HEAD, width), jnp.bfloat16),
            pltpu.VMEM((chips, 8, width), jnp.float32),
            pltpu.VMEM((HEAD, width), jnp.float32),
            pltpu.VMEM((8, width), jnp.float32),
            pltpu.VMEM((requests, width + 4 * ACC, HEAD), jnp.bfloat16),
            pltpu.VMEM((tps, 2 * Q, columns), jnp.bfloat16),
            pltpu.VMEM((tps, 2 * Q, columns), jnp.bfloat16),
            pltpu.VMEM((2, 2 * Q, columns), jnp.bfloat16),
            dma,
            dma((requests,)),
            dma((requests,)),
            dma,
            dma((chips, 2)),
            dma((chips, 2)),
            dma((chips, 2)),
            dma((chips, 2)),
            dma((8,)),
            dma((chips,)),
            dma((requests,)),
            dma((tps,)),
            dma((tps,)),
            dma((2,)),
        ],
        compiler_params=pltpu.CompilerParams(
            collective_id=0, has_side_effects=True, vmem_limit_bytes=40 << 20
        ),
        name="join",
    )(*(pltpu.with_memory_space_constraint(a, pltpu.HBM) for a in (lengths, queries, cache, draft_kv, parents, path, out_weight)))


def solution(mesh):
    chips, tps = mesh.shape["seq"] // 2, mesh.shape["tp"]

    def local(queries, cache, draft_kv, out_weight, lengths, parents, path, accepted):
        attn, chosen, held = join(lengths, queries, cache, draft_kv, parents, path.T, out_weight, chips, tps)
        return commit(lengths, accepted, chosen, attn, held, cache.shape)

    return jax.shard_map(
        local,
        mesh=mesh,
        in_specs=(
            P(None, "tp"),
            P(None, None, "seq", "tp"),
            P(None, "seq", "tp"),
            P("tp", "seq"),
            P(),
            P(),
            P(),
            P(),
        ),
        out_specs=(P("tp", "seq"), P(None, None, "seq", "tp")),
        check_vma=False,
    )
```

```python
import functools

import jax
import jax.numpy as jnp
from jax import lax
from jax.experimental import pallas as pl
from jax.experimental.pallas import tpu as pltpu
from jax.sharding import PartitionSpec as P

HEAD = 128
Q = 64
ACC = 8
MESH = pl.DeviceIdType.MESH
SCALE = HEAD**-0.5 * 1.4426950408889634
DEAD = -1e30
CHUNK = 256
WINDOW = 32


def stacked_heads(rows):
    heads = rows.shape[1] // HEAD
    return jnp.concatenate([rows[:, h * HEAD : (h + 1) * HEAD] for h in range(heads)], axis=0)


def score_chunk(kv, q, c, live):
    s = lax.dot_general(
        kv[0, c * CHUNK : (c + 1) * CHUNK, :], q, (((1,), (1,)), ((), ())), preferred_element_type=jnp.float32
    )
    row = lax.broadcasted_iota(jnp.int32, s.shape, 0) + c * CHUNK
    return jnp.where(row < live, s, DEAD)


def attention_step(now, s_now, peak_now, later, q_later, live, s_later):
    acc = peak = None
    for c in range(s_now.shape[0] // CHUNK):
        rows = slice(c * CHUNK, (c + 1) * CHUNK)
        if later is not None:
            s = score_chunk(later, q_later, c, live)
            s_later[rows, :] = s
            top = jnp.max(s.reshape(CHUNK // 8, 8, s.shape[1]), axis=0)
            peak = top if peak is None else jnp.maximum(peak, top)
        if now is not None:
            p = jnp.exp2(s_now[rows, :] * SCALE - peak_now).astype(jnp.bfloat16)
            values = now[1, rows, :].T
            values = jnp.concatenate([values, jnp.ones((16, CHUNK), values.dtype)], axis=0)
            term = jnp.dot(values, p, preferred_element_type=jnp.float32)
            acc = term if acc is None else acc + term
    if peak is not None:
        peak = jnp.max(peak, axis=0, keepdims=True) * SCALE
    return acc, peak


def publish(o, st, peak, acc):
    o[...] = acc[:HEAD].astype(o.dtype)
    st[0:1] = peak
    st[1:2] = acc[HEAD : HEAD + 1]


def commit_kernel(
    len_ref, acc_ref, chosen_ref, attn_ref, kv_ref, out_ref, nc_ref, win_ref, store_sem, win_sem
):
    requests, span = kv_ref.shape[0], kv_ref.shape[2]
    base = lax.axis_index("seq") * span

    def held(r):
        return (3 - r % 4) * 4 + r // 4

    def place(r):
        off = len_ref[r] - base
        hit = (off + acc_ref[r] > 0) & (off < span)
        return off, hit, pl.multiple_of(jnp.clip(off // 16 * 16, 0, span - WINDOW), 16)

    def store(r):
        return pltpu.make_async_copy(kv_ref.at[held(r)], nc_ref.at[:, r], store_sem.at[r])

    def patch(r, start):
        return pltpu.make_async_copy(win_ref.at[r], nc_ref.at[:, r, pl.ds(start, WINDOW), :], win_sem.at[r])

    def begin(r, _):
        store(r).start()
        return 0

    def change(r, _):
        off, hit, start = place(r)

        @pl.when(hit)
        def _():
            row = lax.broadcasted_iota(jnp.int32, (WINDOW, 2 * ACC), 0) + (start - off)
            node = lax.broadcasted_iota(jnp.int32, (WINDOW, 2 * ACC), 1)
            pick = jnp.where(row == node, 1.0, 0.0).astype(jnp.bfloat16)
            slot = lax.broadcasted_iota(jnp.int32, (WINDOW, HEAD), 0) + (start - off)
            fresh = (slot >= 0) & (slot < acc_ref[r])
            for x in range(2):
                rows = jnp.dot(
                    pick,
                    chosen_ref[r, 2 * ACC * x : 2 * ACC * (x + 1)],
                    preferred_element_type=jnp.float32,
                )
                old = kv_ref[held(r), x, pl.ds(start, WINDOW), :].astype(jnp.float32)
                win_ref[r, x] = jnp.where(fresh, rows, old).astype(jnp.bfloat16)

        return 0

    def end(r, _):
        off, hit, start = place(r)
        store(r).wait()

        @pl.when(hit)
        def _():
            patch(r, start).start()

        return 0

    def close(r, _):
        off, hit, start = place(r)

        @pl.when(hit)
        def _():
            patch(r, start).wait()

        return 0

    lax.fori_loop(0, requests, begin, 0)
    out_ref[...] = attn_ref[...]
    lax.fori_loop(0, requests, change, 0)
    lax.fori_loop(0, requests, end, 0)
    lax.fori_loop(0, requests, close, 0)


def commit(lengths, accepted, chosen, attn, held, shape):
    requests = shape[1]
    near, far = pl.BlockSpec(memory_space=pltpu.VMEM), pl.BlockSpec(memory_space=pl.ANY)
    return pl.pallas_call(
        commit_kernel,
        out_shape=(
            jax.ShapeDtypeStruct(attn.shape, attn.dtype),
            jax.ShapeDtypeStruct(shape, held.dtype),
        ),
        in_specs=[pl.BlockSpec(memory_space=pltpu.SMEM)] * 2 + [near] * 3,
        out_specs=(near, far),
        scratch_shapes=[
            pltpu.VMEM((requests, 2, WINDOW, HEAD), jnp.bfloat16),
            pltpu.SemaphoreType.DMA((requests,)),
            pltpu.SemaphoreType.DMA((requests,)),
        ],
        compiler_params=pltpu.CompilerParams(vmem_limit_bytes=40 << 20),
        name="commit",
    )(lengths, accepted, chosen, attn, held)


def folded_parts(first, second):
    peak = jnp.maximum(first[0], second[0])
    a, b = jnp.exp2(first[0] - peak), jnp.exp2(second[0] - peak)
    return peak, first[1] * a + second[1] * b, a, b


def join_kernel(
    len_ref, q_hbm, kv_hbm, dkv_ref, par_ref, path_ref, w_hbm, out_ref, chosen_ref, kv_ref,
    q_ref, qs_ref, s_ref, peak_ref, o_ref, st_ref, w_ref, pair_o, pair_st, merge_o, merge_st, acc_ref, run_ref, att, rs_send, rs_recv, half_ref,
    q_sem, qs_sem, kv_sem, in_sem, pair_ss, pair_rs, merge_ss, merge_rs, own_ss, pass_ss, att_rs, out_ss, out_rs, half_sem,
):
    s, t = lax.axis_index("seq"), lax.axis_index("tp")
    k, c = s // 2, s % 2
    y, z = k // 4, k % 4
    lx, across = t % 4, (t + 4) % 8
    chips, tps = pair_o.shape[0], rs_send.shape[0]
    partner = 2 * k + 1 - c
    width = o_ref.shape[2]
    heads = width // Q

    barrier = pltpu.get_barrier_semaphore()
    for d in range(1, chips):
        pl.semaphore_signal(barrier, inc=1, device_id={"seq": 2 * ((k + d) % chips) + c}, device_id_type=MESH)
    pl.semaphore_signal(barrier, inc=1, device_id={"seq": partner}, device_id_type=MESH)
    for d in range(1, tps):
        pl.semaphore_signal(barrier, inc=1, device_id={"tp": (t + d) % tps}, device_id_type=MESH)
    span = kv_ref.shape[2]
    jobs = 4 * sum(jnp.where(k < 2**tenant, 1, 0) for tenant in range(4))

    def place(i):
        return 3 - i // 4, i % 4

    def row_of(i):
        tenant, turn = place(i)
        return 4 * turn + tenant

    def live(i):
        return jnp.clip(len_ref[row_of(i)] - s * span, 0, span)

    def qs_load(i):
        rows = pl.ds(pl.multiple_of(row_of(i) * Q, Q), Q)
        return pltpu.make_async_copy(q_hbm.at[rows, :], qs_ref.at[i], qs_sem.at[i])

    def kv_load(i):
        return pltpu.make_async_copy(kv_hbm.at[:, row_of(i)], kv_ref.at[i], kv_sem.at[i])

    q_copy = pltpu.make_async_copy(q_hbm.at[pl.ds(pl.multiple_of(s * Q, Q), Q), :], q_ref, q_sem)
    q_copy.start()

    def start_load(i, _):
        qs_load(i).start()
        kv_load(i).start()
        return 0

    lax.fori_loop(0, jobs, start_load, 0)

    def start_idle(i, _):
        kv_load(i).start()
        return 0

    lax.fori_loop(jobs, kv_ref.shape[0], start_idle, 0)
    w_copy = pltpu.make_async_copy(w_hbm, w_ref, in_sem)
    w_copy.start()

    def send(src, dst, ss, rs, **where):
        return pltpu.make_async_remote_copy(
            src_ref=src, dst_ref=dst, send_sem=ss, recv_sem=rs, device_id=where, device_id_type=MESH
        )

    def pair_copies(j):
        r = 4 * (2 * (j % 2) + 1 - c) + j // 2
        return (
            send(o_ref.at[r], pair_o.at[j], pair_ss.at[j, 0], pair_rs.at[j, 0], seq=partner),
            send(st_ref.at[r, pl.ds(0, 2)], pair_st.at[j, pl.ds(0, 2)], pair_ss.at[j, 1], pair_rs.at[j, 1], seq=partner),
        )

    def merge_copies(j):
        return (
            send(pair_o.at[j], merge_o.at[k], merge_ss.at[j, 0], merge_rs.at[k, 0], seq=2 * j + c),
            send(pair_st.at[j, pl.ds(0, 2)], merge_st.at[k, pl.ds(0, 2)], merge_ss.at[j, 1], merge_rs.at[k, 1], seq=2 * j + c),
        )

    def merge_arrival(i):
        return (
            send(pair_o.at[i], merge_o.at[i], merge_ss.at[i, 0], merge_rs.at[i, 0], seq=partner),
            send(pair_st.at[i, pl.ds(0, 2)], merge_st.at[i, pl.ds(0, 2)], merge_ss.at[i, 1], merge_rs.at[i, 1], seq=partner),
        )

    def pass_on(slot, ss, where):
        return send(att.at[slot], att.at[slot], ss, att_rs.at[slot], seq=where)

    def ring(d):
        return 2 * (y * 4 + (z + d) % 4) + c

    def far_ring(d):
        return 2 * ((1 - y) * 4 + (z + d) % 4) + c

    def out_copy(g):
        slot = jnp.where(g % 2 == 0, t, g // 4 * 4 + lx)
        where = jnp.where(g % 2 == 0, g, t // 4 * 4 + g % 4)
        return send(rs_send.at[g], rs_recv.at[slot], out_ss.at[g], out_rs.at[slot], tp=where)

    def leaves(g):
        return jnp.where(g % 2 == 0, g != t, g % 4 != lx)

    def out_arrival(i):
        return send(rs_send.at[i], rs_recv.at[i], out_ss.at[i], out_rs.at[i], seq=partner)

    def reach_of(j, parity):
        return (1 + 3 * (j % 2)) * (1 + parity)

    node = lax.broadcasted_iota(jnp.int32, (Q, Q), 0)
    other = lax.broadcasted_iota(jnp.int32, (Q, Q), 1)
    parent = jnp.broadcast_to(par_ref[pl.ds(s, 1), :], (Q, Q))
    reach = jnp.where((node == other) | (node == parent), 1.0, 0.0)
    for _ in range((Q - 1).bit_length()):
        bits = reach.astype(jnp.bfloat16)
        reach = jnp.minimum(jnp.dot(bits, bits, preferred_element_type=jnp.float32), 1.0)
    lane = lax.broadcasted_iota(jnp.int32, (Q, width), 1) % Q
    spread = jnp.where(lane == lax.broadcasted_iota(jnp.int32, (Q, width), 0), 1.0, 0.0).astype(jnp.bfloat16)
    alive = jnp.dot(reach.astype(jnp.bfloat16), spread, preferred_element_type=jnp.float32) > 0.5
    q_copy.wait()
    scores = lax.dot_general(
        dkv_ref[0], stacked_heads(q_ref[...]), (((1,), (1,)), ((), ())), preferred_element_type=jnp.float32
    )
    scores = jnp.where(alive, scores, DEAD)
    peak = jnp.max(scores, axis=0, keepdims=True) * SCALE
    weights = jnp.where(alive, jnp.exp2(scores * SCALE - peak), 0.0)
    run_ref[0:1] = peak
    run_ref[1:2] = jnp.sum(weights, axis=0, keepdims=True)
    acc_ref[...] = jnp.dot(dkv_ref[1].T, weights.astype(jnp.bfloat16), preferred_element_type=jnp.float32)

    def combine(tenant, turn):
        pl.when(tenant % 2 == c)(lambda: combine_now(tenant, turn))

    def combine_now(tenant, turn):
        j = 2 * turn + tenant // 2
        r = 4 * tenant + turn
        for copy in pair_copies(j):
            copy.wait_recv()
        peak, total, a, b = folded_parts((st_ref[r, 0:1], st_ref[r, 1:2]), (pair_st[j, 0:1], pair_st[j, 1:2]))
        mixed = o_ref[r].astype(jnp.float32) * a + pair_o[j].astype(jnp.float32) * b
        pair_o[j] = mixed.astype(jnp.bfloat16)
        pair_st[j, 0:1] = peak
        pair_st[j, 1:2] = total

        @pl.when(j != k)
        def _():
            for copy in merge_copies(j):
                copy.start()

    def start_pair(tenant, turn):
        @pl.when(tenant % 2 != c)
        def _():
            for copy in pair_copies(2 * turn + tenant // 2):
                copy.start()

    qs_load(0).wait()
    kv_load(0).wait()
    _, above = attention_step(
        None, s_ref.at[0], None, kv_ref.at[0], stacked_heads(qs_ref[0]), live(0), s_ref.at[0]
    )
    peak_ref[0:1] = above
    def attend_two(n):
        for u in range(2):
            now = 2 * n + u
            later = jnp.where(now + 1 < jobs, now + 1, 0)

            @pl.when(now + 1 < jobs)
            def _():
                qs_load(later).wait()
                kv_load(later).wait()

            peak = peak_ref[u : u + 1]
            acc, above = attention_step(
                kv_ref.at[now], s_ref.at[u], peak,
                kv_ref.at[later], stacked_heads(qs_ref[later]), live(later), s_ref.at[1 - u],
            )
            tenant, turn = place(now)
            publish(o_ref.at[4 * tenant + turn], st_ref.at[4 * tenant + turn], peak, acc)
            peak_ref[1 - u : 2 - u] = above

    attend_two(0)
    pl.semaphore_wait(barrier, chips + tps - 1)

    def start_two(n):
        for u in range(2):
            start_pair(*place(2 * n + u))

    start_two(0)

    def attend_pair(n, _):
        attend_two(n)
        start_two(n)

        for u in range(2):
            combine(*place(2 * n - 2 + u))
        return 0

    lax.fori_loop(1, jobs // 2, attend_pair, 0)
    for u in range(2):
        combine(*place(jobs - 2 + u))

    def absorb(o, st):
        peak, total, a, b = folded_parts((run_ref[0:1], run_ref[1:2]), (st[0:1], st[1:2]))
        acc_ref[...] = acc_ref[...] * a + o[...].astype(jnp.float32) * b
        run_ref[0:1] = peak
        run_ref[1:2] = total

    def merge(i, _):
        j = (k + i) % chips

        @pl.when(j < reach_of(k, c))
        def _():
            @pl.when(j == k)
            def _():
                absorb(pair_o.at[j], pair_st.at[j])

            @pl.when(j != k)
            def _():
                for copy in merge_arrival(j):
                    copy.wait_recv()
                absorb(merge_o.at[j], merge_st.at[j])

        return 0

    lax.fori_loop(0, chips, merge, 0)

    att[s, :width] = (acc_ref[...] / run_ref[1:2]).T.astype(jnp.bfloat16)
    lanes = lax.broadcasted_iota(jnp.int32, path_ref.shape, 1)
    nodes = jnp.sum(jnp.where(lanes == s, path_ref[...], 0), axis=1, keepdims=True)
    pick = jnp.where(lax.broadcasted_iota(jnp.int32, (ACC, Q), 1) == nodes, 1.0, 0.0)
    pick = jnp.concatenate([pick, jnp.zeros((ACC, Q), jnp.float32)], axis=0).astype(jnp.bfloat16)
    for x in range(2):
        rows = jnp.dot(pick, dkv_ref[x], preferred_element_type=jnp.float32)
        att[s, width + 2 * ACC * x : width + 2 * ACC * (x + 1)] = rows.astype(jnp.bfloat16)

    twin = (k + 4) % chips
    own = [pass_on(s, own_ss.at[0], 2 * twin + c)]
    own += [pass_on(s, own_ss.at[d], ring(d)) for d in (1, 3, 2)]
    own += [pass_on(s, own_ss.at[4], partner)]
    own += [pass_on(s, own_ss.at[4 + d], far_ring(d)) for d in (1, 3, 2)]
    for copy in own:
        copy.start()

    def group(i):
        return (y + i // 2) % 2 * 4 + (z // 2 * 2 + 2 * i + 1 - i // 4) % 4

    def forward(g):
        return pass_on(2 * g + c, pass_ss.at[g], partner)

    def arrival(slot):
        return pass_on(slot, own_ss.at[0], partner)

    def project(g):
        arrival(2 * g + 1 - c).wait_recv()
        rows = jnp.concatenate(
            [
                jnp.concatenate([att[2 * g, h * Q : (h + 1) * Q], att[2 * g + 1, h * Q : (h + 1) * Q]], axis=0)
                for h in range(heads)
            ],
            axis=1,
        )
        rs_send[g] = jnp.dot(rows, w_ref[...], preferred_element_type=jnp.float32).astype(jnp.bfloat16)

        @pl.when(leaves(g))
        def _():
            out_copy(g).start()

    def spread_on(i, _):
        g = group(i)

        @pl.when(g != k)
        def _():
            arrival(2 * g + c).wait_recv()
            forward(g).start()

        @pl.when(i > 0)
        def _():
            project(group(i - 1))

        return 0

    w_copy.wait()
    lax.fori_loop(0, chips, spread_on, 0)
    project(group(chips - 1))

    def gathered(g, slots):
        total = rs_send[g].astype(jnp.float32)
        for i in slots:
            out_arrival(i).wait_recv()
            total = total + rs_recv[i].astype(jnp.float32)
        return total

    def row_slots(g):
        return [g // 4 * 4 + (lx + d) % 4 for d in range(1, 4)]

    swap = send(half_ref.at[0], half_ref.at[1], half_sem.at[0], half_sem.at[1], tp=across)

    @pl.when(t % 2 == 1)
    def _():
        half_ref[0] = gathered(across, row_slots(across)).astype(jnp.bfloat16)
        swap.start()
        total = gathered(t, row_slots(t))
        swap.wait()
        out_ref[...] = (total + half_ref[1].astype(jnp.float32)).astype(out_ref.dtype)

    @pl.when(t % 2 == 0)
    def _():
        out_ref[...] = gathered(t, [(t + d) % tps for d in range(1, tps)]).astype(out_ref.dtype)

    chosen_ref[...] = att[:, width:]

    def finish_pair(j, _):
        @pl.when(k < reach_of(j, 1 - c))
        def _():
            for copy in pair_copies(j):
                copy.wait_send()

        @pl.when((k < reach_of(j, c)) & (j != k))
        def _():
            for copy in merge_copies(j):
                copy.wait_send()

        @pl.when(j != k)
        def _():
            forward(j).wait_send()

        @pl.when(leaves(j))
        def _():
            out_copy(j).wait_send()

        return 0

    lax.fori_loop(0, chips, finish_pair, 0)

    def finish_idle(i, _):
        kv_load(i).wait()
        return 0

    lax.fori_loop(jobs, kv_ref.shape[0], finish_idle, 0)
    for copy in own:
        copy.wait_send()


def join(lengths, queries, cache, draft_kv, parents, path, out_weight, chips, tps):
    requests, span = cache.shape[1], cache.shape[2]
    wide, columns = queries.shape[1], out_weight.shape[1]
    width = wide // HEAD * Q
    dma = pltpu.SemaphoreType.DMA
    whole, far = pl.BlockSpec(memory_space=pltpu.VMEM), pl.BlockSpec(memory_space=pl.ANY)
    return pl.pallas_call(
        join_kernel,
        out_shape=(
            jax.ShapeDtypeStruct((queries.shape[0] // tps, columns), jnp.bfloat16),
            jax.ShapeDtypeStruct((requests, 4 * ACC, HEAD), jnp.bfloat16),
            jax.ShapeDtypeStruct((requests, 2, span, HEAD), jnp.bfloat16),
        ),
        in_specs=[pl.BlockSpec(memory_space=pltpu.SMEM), far, far, whole, whole, whole, far],
        out_specs=(whole, whole, whole),
        scratch_shapes=[
            pltpu.VMEM((Q, wide), jnp.bfloat16),
            pltpu.VMEM((requests, Q, wide), jnp.bfloat16),
            pltpu.VMEM((2, span, width), jnp.float32),
            pltpu.VMEM((8, width), jnp.float32),
            pltpu.VMEM((requests, HEAD, width), jnp.bfloat16),
            pltpu.VMEM((requests, 8, width), jnp.float32),
            pltpu.VMEM(out_weight.shape, out_weight.dtype),
            pltpu.VMEM((chips, HEAD, width), jnp.bfloat16),
            pltpu.VMEM((chips, 8, width), jnp.float32),
            pltpu.VMEM((chips, HEAD, width), jnp.bfloat16),
            pltpu.VMEM((chips, 8, width), jnp.float32),
            pltpu.VMEM((HEAD, width), jnp.float32),
            pltpu.VMEM((8, width), jnp.float32),
            pltpu.VMEM((requests, width + 4 * ACC, HEAD), jnp.bfloat16),
            pltpu.VMEM((tps, 2 * Q, columns), jnp.bfloat16),
            pltpu.VMEM((tps, 2 * Q, columns), jnp.bfloat16),
            pltpu.VMEM((2, 2 * Q, columns), jnp.bfloat16),
            dma,
            dma((requests,)),
            dma((requests,)),
            dma,
            dma((chips, 2)),
            dma((chips, 2)),
            dma((chips, 2)),
            dma((chips, 2)),
            dma((8,)),
            dma((chips,)),
            dma((requests,)),
            dma((tps,)),
            dma((tps,)),
            dma((2,)),
        ],
        compiler_params=pltpu.CompilerParams(
            collective_id=0, has_side_effects=True, vmem_limit_bytes=40 << 20
        ),
        name="join",
    )(*(pltpu.with_memory_space_constraint(a, pltpu.HBM) for a in (lengths, queries, cache, draft_kv, parents, path, out_weight)))


def solution(mesh):
    chips, tps = mesh.shape["seq"] // 2, mesh.shape["tp"]

    def local(queries, cache, draft_kv, out_weight, lengths, parents, path, accepted):
        attn, chosen, held = join(lengths, queries, cache, draft_kv, parents, path.T, out_weight, chips, tps)
        return commit(lengths, accepted, chosen, attn, held, cache.shape)

    return jax.shard_map(
        local,
        mesh=mesh,
        in_specs=(
            P(None, "tp"),
            P(None, None, "seq", "tp"),
            P(None, "seq", "tp"),
            P("tp", "seq"),
            P(),
            P(),
            P(),
            P(),
        ),
        out_specs=(P("tp", "seq"), P(None, None, "seq", "tp")),
        check_vma=False,
    )
```

```python
import functools

import jax
import jax.numpy as jnp
from jax import lax
from jax.experimental import pallas as pl
from jax.experimental.pallas import tpu as pltpu
from jax.sharding import PartitionSpec as P

HEAD = 128
Q = 64
ACC = 8
MESH = pl.DeviceIdType.MESH
SCALE = HEAD**-0.5 * 1.4426950408889634
DEAD = -1e30
CHUNK = 256
WINDOW = 32


def stacked_heads(rows):
    heads = rows.shape[1] // HEAD
    return jnp.concatenate([rows[:, h * HEAD : (h + 1) * HEAD] for h in range(heads)], axis=0)


def score_chunk(kv, q, c, live):
    s = lax.dot_general(
        kv[0, c * CHUNK : (c + 1) * CHUNK, :], q, (((1,), (1,)), ((), ())), preferred_element_type=jnp.float32
    )
    if live is None:
        return s
    row = lax.broadcasted_iota(jnp.int32, s.shape, 0) + c * CHUNK
    return jnp.where(row < live, s, DEAD)


def attention_step(now, s_now, peak_now, later, q_later, live, s_later):
    acc = peak = None
    for c in range(s_now.shape[0] // CHUNK):
        rows = slice(c * CHUNK, (c + 1) * CHUNK)
        if later is not None:
            s = score_chunk(later, q_later, c, live)
            s_later[rows, :] = s
            top = jnp.max(s.reshape(CHUNK // 8, 8, s.shape[1]), axis=0)
            peak = top if peak is None else jnp.maximum(peak, top)
        if now is not None:
            p = jnp.exp2(s_now[rows, :] * SCALE - peak_now).astype(jnp.bfloat16)
            values = now[1, rows, :].T
            values = jnp.concatenate([values, jnp.ones((16, CHUNK), values.dtype)], axis=0)
            term = jnp.dot(values, p, preferred_element_type=jnp.float32)
            acc = term if acc is None else acc + term
    if peak is not None:
        peak = jnp.max(peak, axis=0, keepdims=True) * SCALE
    return acc, peak


def publish(o, st, peak, acc):
    o[...] = acc[:HEAD].astype(o.dtype)
    st[0:1] = peak
    st[1:2] = acc[HEAD : HEAD + 1]


def commit_kernel(
    len_ref, acc_ref, chosen_ref, attn_ref, kv_ref, out_ref, nc_ref, win_ref, store_sem, win_sem
):
    requests, span = kv_ref.shape[0], kv_ref.shape[2]
    base = lax.axis_index("seq") * span

    def held(r):
        return (3 - r % 4) * 4 + r // 4

    def place(r):
        off = len_ref[r] - base
        hit = (off + acc_ref[r] > 0) & (off < span)
        return off, hit, pl.multiple_of(jnp.clip(off // 16 * 16, 0, span - WINDOW), 16)

    def store(r):
        return pltpu.make_async_copy(kv_ref.at[held(r)], nc_ref.at[:, r], store_sem.at[r])

    def patch(r, start):
        return pltpu.make_async_copy(win_ref.at[r], nc_ref.at[:, r, pl.ds(start, WINDOW), :], win_sem.at[r])

    def begin(r, _):
        store(r).start()
        return 0

    def change(r, _):
        off, hit, start = place(r)

        @pl.when(hit)
        def _():
            row = lax.broadcasted_iota(jnp.int32, (WINDOW, 2 * ACC), 0) + (start - off)
            node = lax.broadcasted_iota(jnp.int32, (WINDOW, 2 * ACC), 1)
            pick = jnp.where(row == node, 1.0, 0.0).astype(jnp.bfloat16)
            slot = lax.broadcasted_iota(jnp.int32, (WINDOW, HEAD), 0) + (start - off)
            fresh = (slot >= 0) & (slot < acc_ref[r])
            for x in range(2):
                rows = jnp.dot(
                    pick,
                    chosen_ref[r, 2 * ACC * x : 2 * ACC * (x + 1)],
                    preferred_element_type=jnp.float32,
                )
                old = kv_ref[held(r), x, pl.ds(start, WINDOW), :].astype(jnp.float32)
                win_ref[r, x] = jnp.where(fresh, rows, old).astype(jnp.bfloat16)

        return 0

    def end(r, _):
        off, hit, start = place(r)
        store(r).wait()

        @pl.when(hit)
        def _():
            patch(r, start).start()

        return 0

    def close(r, _):
        off, hit, start = place(r)

        @pl.when(hit)
        def _():
            patch(r, start).wait()

        return 0

    lax.fori_loop(0, requests, begin, 0)
    out_ref[...] = attn_ref[...]
    lax.fori_loop(0, requests, change, 0)
    lax.fori_loop(0, requests, end, 0)
    lax.fori_loop(0, requests, close, 0)


def commit(lengths, accepted, chosen, attn, held, shape):
    requests = shape[1]
    near, far = pl.BlockSpec(memory_space=pltpu.VMEM), pl.BlockSpec(memory_space=pl.ANY)
    return pl.pallas_call(
        commit_kernel,
        out_shape=(
            jax.ShapeDtypeStruct(attn.shape, attn.dtype),
            jax.ShapeDtypeStruct(shape, held.dtype),
        ),
        in_specs=[pl.BlockSpec(memory_space=pltpu.SMEM)] * 2 + [near] * 3,
        out_specs=(near, far),
        scratch_shapes=[
            pltpu.VMEM((requests, 2, WINDOW, HEAD), jnp.bfloat16),
            pltpu.SemaphoreType.DMA((requests,)),
            pltpu.SemaphoreType.DMA((requests,)),
        ],
        compiler_params=pltpu.CompilerParams(vmem_limit_bytes=40 << 20),
        name="commit",
    )(lengths, accepted, chosen, attn, held)


def folded_parts(first, second):
    peak = jnp.maximum(first[0], second[0])
    a, b = jnp.exp2(first[0] - peak), jnp.exp2(second[0] - peak)
    return peak, first[1] * a + second[1] * b, a, b


def join_kernel(
    len_ref, q_hbm, kv_hbm, dkv_ref, par_ref, path_ref, w_hbm, out_ref, chosen_ref, kv_ref,
    q_ref, qs_ref, s_ref, peak_ref, o_ref, st_ref, w_ref, pair_o, pair_st, merge_o, merge_st, acc_ref, run_ref, att, rs_send, rs_recv, half_ref,
    q_sem, qs_sem, kv_sem, in_sem, pair_ss, pair_rs, merge_ss, merge_rs, own_ss, pass_ss, att_rs, out_ss, out_rs, half_sem,
):
    s, t = lax.axis_index("seq"), lax.axis_index("tp")
    k, c = s // 2, s % 2
    y, z = k // 4, k % 4
    lx, across = t % 4, (t + 4) % 8
    chips, tps = pair_o.shape[0], rs_send.shape[0]
    partner = 2 * k + 1 - c
    width = o_ref.shape[2]
    heads = width // Q

    barrier = pltpu.get_barrier_semaphore()
    for d in range(1, chips):
        pl.semaphore_signal(barrier, inc=1, device_id={"seq": 2 * ((k + d) % chips) + c}, device_id_type=MESH)
    pl.semaphore_signal(barrier, inc=1, device_id={"seq": partner}, device_id_type=MESH)
    for d in range(1, tps):
        pl.semaphore_signal(barrier, inc=1, device_id={"tp": (t + d) % tps}, device_id_type=MESH)
    span = kv_ref.shape[2]
    jobs = 4 * sum(jnp.where(k < 2**tenant, 1, 0) for tenant in range(4))

    def place(i):
        return 3 - i // 4, i % 4

    def row_of(i):
        tenant, turn = place(i)
        return 4 * turn + tenant

    def live(i):
        return jnp.clip(len_ref[row_of(i)] - s * span, 0, span)

    def qs_load(i):
        rows = pl.ds(pl.multiple_of(row_of(i) * Q, Q), Q)
        return pltpu.make_async_copy(q_hbm.at[rows, :], qs_ref.at[i], qs_sem.at[i])

    def kv_load(i):
        return pltpu.make_async_copy(kv_hbm.at[:, row_of(i)], kv_ref.at[i], kv_sem.at[i])

    q_copy = pltpu.make_async_copy(q_hbm.at[pl.ds(pl.multiple_of(s * Q, Q), Q), :], q_ref, q_sem)
    q_copy.start()

    def start_load(i, _):
        qs_load(i).start()
        kv_load(i).start()
        return 0

    lax.fori_loop(0, jobs, start_load, 0)

    def start_idle(i, _):
        kv_load(i).start()
        return 0

    lax.fori_loop(jobs, kv_ref.shape[0], start_idle, 0)
    w_copy = pltpu.make_async_copy(w_hbm, w_ref, in_sem)
    w_copy.start()

    def send(src, dst, ss, rs, **where):
        return pltpu.make_async_remote_copy(
            src_ref=src, dst_ref=dst, send_sem=ss, recv_sem=rs, device_id=where, device_id_type=MESH
        )

    def pair_copies(j):
        r = 4 * (2 * (j % 2) + 1 - c) + j // 2
        return (
            send(o_ref.at[r], pair_o.at[j], pair_ss.at[j, 0], pair_rs.at[j, 0], seq=partner),
            send(st_ref.at[r, pl.ds(0, 2)], pair_st.at[j, pl.ds(0, 2)], pair_ss.at[j, 1], pair_rs.at[j, 1], seq=partner),
        )

    def merge_copies(j):
        return (
            send(pair_o.at[j], merge_o.at[k], merge_ss.at[j, 0], merge_rs.at[k, 0], seq=2 * j + c),
            send(pair_st.at[j, pl.ds(0, 2)], merge_st.at[k, pl.ds(0, 2)], merge_ss.at[j, 1], merge_rs.at[k, 1], seq=2 * j + c),
        )

    def merge_arrival(i):
        return (
            send(pair_o.at[i], merge_o.at[i], merge_ss.at[i, 0], merge_rs.at[i, 0], seq=partner),
            send(pair_st.at[i, pl.ds(0, 2)], merge_st.at[i, pl.ds(0, 2)], merge_ss.at[i, 1], merge_rs.at[i, 1], seq=partner),
        )

    def pass_on(slot, ss, where):
        return send(att.at[slot], att.at[slot], ss, att_rs.at[slot], seq=where)

    def ring(d):
        return 2 * (y * 4 + (z + d) % 4) + c

    def far_ring(d):
        return 2 * ((1 - y) * 4 + (z + d) % 4) + c

    def out_copy(g):
        slot = jnp.where(g % 2 == 0, t, g // 4 * 4 + lx)
        where = jnp.where(g % 2 == 0, g, t // 4 * 4 + g % 4)
        return send(rs_send.at[g], rs_recv.at[slot], out_ss.at[g], out_rs.at[slot], tp=where)

    def leaves(g):
        return jnp.where(g % 2 == 0, g != t, g % 4 != lx)

    def out_arrival(i):
        return send(rs_send.at[i], rs_recv.at[i], out_ss.at[i], out_rs.at[i], seq=partner)

    def reach_of(j, parity):
        return (1 + 3 * (j % 2)) * (1 + parity)

    node = lax.broadcasted_iota(jnp.int32, (Q, Q), 0)
    other = lax.broadcasted_iota(jnp.int32, (Q, Q), 1)
    parent = jnp.broadcast_to(par_ref[pl.ds(s, 1), :], (Q, Q))
    reach = jnp.where((node == other) | (node == parent), 1.0, 0.0)
    for _ in range((Q - 1).bit_length()):
        bits = reach.astype(jnp.bfloat16)
        reach = jnp.minimum(jnp.dot(bits, bits, preferred_element_type=jnp.float32), 1.0)
    lane = lax.broadcasted_iota(jnp.int32, (Q, width), 1) % Q
    spread = jnp.where(lane == lax.broadcasted_iota(jnp.int32, (Q, width), 0), 1.0, 0.0).astype(jnp.bfloat16)
    alive = jnp.dot(reach.astype(jnp.bfloat16), spread, preferred_element_type=jnp.float32) > 0.5
    q_copy.wait()
    scores = lax.dot_general(
        dkv_ref[0], stacked_heads(q_ref[...]), (((1,), (1,)), ((), ())), preferred_element_type=jnp.float32
    )
    scores = jnp.where(alive, scores, DEAD)
    peak = jnp.max(scores, axis=0, keepdims=True) * SCALE
    weights = jnp.where(alive, jnp.exp2(scores * SCALE - peak), 0.0)
    run_ref[0:1] = peak
    run_ref[1:2] = jnp.sum(weights, axis=0, keepdims=True)
    acc_ref[...] = jnp.dot(dkv_ref[1].T, weights.astype(jnp.bfloat16), preferred_element_type=jnp.float32)

    def combine(tenant, turn):
        pl.when(tenant % 2 == c)(lambda: combine_now(tenant, turn))

    def combine_now(tenant, turn):
        j = 2 * turn + tenant // 2
        r = 4 * tenant + turn
        for copy in pair_copies(j):
            copy.wait_recv()
        peak, total, a, b = folded_parts((st_ref[r, 0:1], st_ref[r, 1:2]), (pair_st[j, 0:1], pair_st[j, 1:2]))
        mixed = o_ref[r].astype(jnp.float32) * a + pair_o[j].astype(jnp.float32) * b
        pair_o[j] = mixed.astype(jnp.bfloat16)
        pair_st[j, 0:1] = peak
        pair_st[j, 1:2] = total

        @pl.when(j != k)
        def _():
            for copy in merge_copies(j):
                copy.start()

    def start_pair(tenant, turn):
        @pl.when(tenant % 2 != c)
        def _():
            for copy in pair_copies(2 * turn + tenant // 2):
                copy.start()

    qs_load(0).wait()
    kv_load(0).wait()
    _, above = attention_step(
        None, s_ref.at[0], None, kv_ref.at[0], stacked_heads(qs_ref[0]), live(0), s_ref.at[0]
    )
    peak_ref[0:1] = above
    def attend_one(n, u, masked=True, ahead=True):
        now = 2 * n + u
        peak = peak_ref[u : u + 1]
        if ahead:
            later = now + 1
            qs_load(later).wait()
            kv_load(later).wait()
            acc, above = attention_step(
                kv_ref.at[now], s_ref.at[u], peak,
                kv_ref.at[later], stacked_heads(qs_ref[later]), live(later) if masked else None, s_ref.at[1 - u],
            )
            peak_ref[1 - u : 2 - u] = above
        else:
            acc, _ = attention_step(kv_ref.at[now], s_ref.at[u], peak, None, None, None, None)
        tenant, turn = place(now)
        publish(o_ref.at[4 * tenant + turn], st_ref.at[4 * tenant + turn], peak, acc)

    for u in range(2):
        attend_one(0, u)
    pl.semaphore_wait(barrier, chips + tps - 1)
    for u in range(2):
        start_pair(*place(u))

    def attend_pair(n, masked=True, last=False):
        for u in range(2):
            attend_one(n, u, masked, not last or u == 0)
            start_pair(*place(2 * n + u))
        for u in range(2):
            combine(*place(2 * n - 2 + u))
        return 0

    full = 4 * sum(jnp.where(s + 1 < 2**tenant, 1, 0) for tenant in range(4))
    full, pairs = jnp.maximum(full // 2 - 1, 1), jobs // 2
    lax.fori_loop(1, full, lambda n, _: attend_pair(n, masked=False), 0)
    lax.fori_loop(full, pairs - 1, lambda n, _: attend_pair(n), 0)
    attend_pair(pairs - 1, last=True)
    for u in range(2):
        combine(*place(jobs - 2 + u))

    def absorb(o, st):
        peak, total, a, b = folded_parts((run_ref[0:1], run_ref[1:2]), (st[0:1], st[1:2]))
        acc_ref[...] = acc_ref[...] * a + o[...].astype(jnp.float32) * b
        run_ref[0:1] = peak
        run_ref[1:2] = total

    def merge(i, _):
        j = (k + i) % chips

        @pl.when(j < reach_of(k, c))
        def _():
            @pl.when(j == k)
            def _():
                absorb(pair_o.at[j], pair_st.at[j])

            @pl.when(j != k)
            def _():
                for copy in merge_arrival(j):
                    copy.wait_recv()
                absorb(merge_o.at[j], merge_st.at[j])

        return 0

    lax.fori_loop(0, chips, merge, 0)

    att[s, :width] = (acc_ref[...] / run_ref[1:2]).T.astype(jnp.bfloat16)
    lanes = lax.broadcasted_iota(jnp.int32, path_ref.shape, 1)
    nodes = jnp.sum(jnp.where(lanes == s, path_ref[...], 0), axis=1, keepdims=True)
    pick = jnp.where(lax.broadcasted_iota(jnp.int32, (ACC, Q), 1) == nodes, 1.0, 0.0)
    pick = jnp.concatenate([pick, jnp.zeros((ACC, Q), jnp.float32)], axis=0).astype(jnp.bfloat16)
    for x in range(2):
        rows = jnp.dot(pick, dkv_ref[x], preferred_element_type=jnp.float32)
        att[s, width + 2 * ACC * x : width + 2 * ACC * (x + 1)] = rows.astype(jnp.bfloat16)

    twin = (k + 4) % chips
    own = [pass_on(s, own_ss.at[0], 2 * twin + c)]
    own += [pass_on(s, own_ss.at[d], ring(d)) for d in (1, 3, 2)]
    own += [pass_on(s, own_ss.at[4], partner)]
    own += [pass_on(s, own_ss.at[4 + d], far_ring(d)) for d in (1, 3, 2)]
    for copy in own:
        copy.start()

    def group(i):
        return (y + i // 2) % 2 * 4 + (z // 2 * 2 + 2 * i + 1 - i // 4) % 4

    def forward(g):
        return pass_on(2 * g + c, pass_ss.at[g], partner)

    def arrival(slot):
        return pass_on(slot, own_ss.at[0], partner)

    def project(g):
        arrival(2 * g + 1 - c).wait_recv()
        rows = jnp.concatenate(
            [
                jnp.concatenate([att[2 * g, h * Q : (h + 1) * Q], att[2 * g + 1, h * Q : (h + 1) * Q]], axis=0)
                for h in range(heads)
            ],
            axis=1,
        )
        rs_send[g] = jnp.dot(rows, w_ref[...], preferred_element_type=jnp.float32).astype(jnp.bfloat16)

        @pl.when(leaves(g))
        def _():
            out_copy(g).start()

    def spread_on(i, _):
        g = group(i)

        @pl.when(g != k)
        def _():
            arrival(2 * g + c).wait_recv()
            forward(g).start()

        @pl.when(i > 0)
        def _():
            project(group(i - 1))

        return 0

    w_copy.wait()
    lax.fori_loop(0, chips, spread_on, 0)
    project(group(chips - 1))

    def gathered(g, slots):
        total = rs_send[g].astype(jnp.float32)
        for i in slots:
            out_arrival(i).wait_recv()
            total = total + rs_recv[i].astype(jnp.float32)
        return total

    def row_slots(g):
        return [g // 4 * 4 + (lx + d) % 4 for d in range(1, 4)]

    swap = send(half_ref.at[0], half_ref.at[1], half_sem.at[0], half_sem.at[1], tp=across)

    @pl.when(t % 2 == 1)
    def _():
        half_ref[0] = gathered(across, row_slots(across)).astype(jnp.bfloat16)
        swap.start()
        total = gathered(t, row_slots(t))
        swap.wait()
        out_ref[...] = (total + half_ref[1].astype(jnp.float32)).astype(out_ref.dtype)

    @pl.when(t % 2 == 0)
    def _():
        out_ref[...] = gathered(t, [(t + d) % tps for d in range(1, tps)]).astype(out_ref.dtype)

    chosen_ref[...] = att[:, width:]

    def finish_pair(j, _):
        @pl.when(k < reach_of(j, 1 - c))
        def _():
            for copy in pair_copies(j):
                copy.wait_send()

        @pl.when((k < reach_of(j, c)) & (j != k))
        def _():
            for copy in merge_copies(j):
                copy.wait_send()

        @pl.when(j != k)
        def _():
            forward(j).wait_send()

        @pl.when(leaves(j))
        def _():
            out_copy(j).wait_send()

        return 0

    lax.fori_loop(0, chips, finish_pair, 0)

    def finish_idle(i, _):
        kv_load(i).wait()
        return 0

    lax.fori_loop(jobs, kv_ref.shape[0], finish_idle, 0)
    for copy in own:
        copy.wait_send()


def join(lengths, queries, cache, draft_kv, parents, path, out_weight, chips, tps):
    requests, span = cache.shape[1], cache.shape[2]
    wide, columns = queries.shape[1], out_weight.shape[1]
    width = wide // HEAD * Q
    dma = pltpu.SemaphoreType.DMA
    whole, far = pl.BlockSpec(memory_space=pltpu.VMEM), pl.BlockSpec(memory_space=pl.ANY)
    return pl.pallas_call(
        join_kernel,
        out_shape=(
            jax.ShapeDtypeStruct((queries.shape[0] // tps, columns), jnp.bfloat16),
            jax.ShapeDtypeStruct((requests, 4 * ACC, HEAD), jnp.bfloat16),
            jax.ShapeDtypeStruct((requests, 2, span, HEAD), jnp.bfloat16),
        ),
        in_specs=[pl.BlockSpec(memory_space=pltpu.SMEM), far, far, whole, whole, whole, far],
        out_specs=(whole, whole, whole),
        scratch_shapes=[
            pltpu.VMEM((Q, wide), jnp.bfloat16),
            pltpu.VMEM((requests, Q, wide), jnp.bfloat16),
            pltpu.VMEM((2, span, width), jnp.float32),
            pltpu.VMEM((8, width), jnp.float32),
            pltpu.VMEM((requests, HEAD, width), jnp.bfloat16),
            pltpu.VMEM((requests, 8, width), jnp.float32),
            pltpu.VMEM(out_weight.shape, out_weight.dtype),
            pltpu.VMEM((chips, HEAD, width), jnp.bfloat16),
            pltpu.VMEM((chips, 8, width), jnp.float32),
            pltpu.VMEM((chips, HEAD, width), jnp.bfloat16),
            pltpu.VMEM((chips, 8, width), jnp.float32),
            pltpu.VMEM((HEAD, width), jnp.float32),
            pltpu.VMEM((8, width), jnp.float32),
            pltpu.VMEM((requests, width + 4 * ACC, HEAD), jnp.bfloat16),
            pltpu.VMEM((tps, 2 * Q, columns), jnp.bfloat16),
            pltpu.VMEM((tps, 2 * Q, columns), jnp.bfloat16),
            pltpu.VMEM((2, 2 * Q, columns), jnp.bfloat16),
            dma,
            dma((requests,)),
            dma((requests,)),
            dma,
            dma((chips, 2)),
            dma((chips, 2)),
            dma((chips, 2)),
            dma((chips, 2)),
            dma((8,)),
            dma((chips,)),
            dma((requests,)),
            dma((tps,)),
            dma((tps,)),
            dma((2,)),
        ],
        compiler_params=pltpu.CompilerParams(
            collective_id=0, has_side_effects=True, vmem_limit_bytes=40 << 20
        ),
        name="join",
    )(*(pltpu.with_memory_space_constraint(a, pltpu.HBM) for a in (lengths, queries, cache, draft_kv, parents, path, out_weight)))


def solution(mesh):
    chips, tps = mesh.shape["seq"] // 2, mesh.shape["tp"]

    def local(queries, cache, draft_kv, out_weight, lengths, parents, path, accepted):
        attn, chosen, held = join(lengths, queries, cache, draft_kv, parents, path.T, out_weight, chips, tps)
        return commit(lengths, accepted, chosen, attn, held, cache.shape)

    return jax.shard_map(
        local,
        mesh=mesh,
        in_specs=(
            P(None, "tp"),
            P(None, None, "seq", "tp"),
            P(None, "seq", "tp"),
            P("tp", "seq"),
            P(),
            P(),
            P(),
            P(),
        ),
        out_specs=(P("tp", "seq"), P(None, None, "seq", "tp")),
        check_vma=False,
    )
```
